32 devices in a mesh: dp: 16 (over z, y, x), mp: 2 (over core).
Axes of the slice: x: 2, y: 2, z: 4, core: 2. Of those that a mesh axis runs over, the one named last changes fastest.
Arguments:
- residual: bfloat16 [256, 4608], P(None, 'dp'), may hold values from -60 to 60
- norm_gain: float32 [4608], P('dp'), may hold values from 0.25 to 1.75
- query_weight: bfloat16 [4608, 2048], P('dp', 'mp'), may hold values from -2 to 2
- key_weight: bfloat16 [4608, 1024], P('dp', 'mp'), may hold values from -2 to 2
- value_weight: bfloat16 [4608, 1024], P('dp', 'mp'), may hold values from -0.09375 to 0.09375
- out_weight: bfloat16 [2048, 4608], P('mp', 'dp'), may hold values from -1 to 1
- post_gain: float32 [4608], P('dp'), may hold values from 0.25 to 1.75
- encoder_weight: bfloat16 [4608, 8192], P(None, ('dp', 'mp')), may hold values from -0.09375 to 0.09375
- encoder_bias: float32 [8192], P(('dp', 'mp')), may hold values from -3 to 3
- decoder_weight: bfloat16 [8192, 4608], P(('dp', 'mp')), may hold values from -0.125 to 0.125
- decoder_bias: float32 [4608], replicated, may hold values from -3 to 3
Outputs:
- encoder_grad: bfloat16 [4608, 8192], P(None, ('dp', 'mp'))
- encoder_bias_grad: float32 [8192], P(('dp', 'mp'))
- decoder_grad: bfloat16 [8192, 4608], P(('dp', 'mp'))
The draws below stay inside these ranges and needn't reach their ends.
All inputs are finite; a program needn't handle non-finite values.
Results may differ from the reference program's by a relative error of at most 0.015.
Values may be sent and summed in bfloat16 or wider, within the bound.
No kernel may reach another device: no remote copies, remote signals or barrier semaphores. Data moves between devices by JAX's collectives and lax.ppermute only.
A program may use at most 128 MiB of HBM per device.

```python
import jax
import jax.numpy as jnp
from jax import lax

D = 4608
HEADS = 16
KV_HEADS = 8
HEAD_DIM = 128
TOKENS = 256
LATENTS = 8192


def draw_residual(key, part):
    key_noise = jax.random.fold_in(key, 11)
    key_rows = jax.random.fold_in(key, 12)
    columns = jnp.arange(D, dtype=jnp.float32) / D
    sample = jax.random.truncated_normal(key_noise, -4.0, 4.0, (TOKENS, D), jnp.float32)
    row_scale = 10.0 ** jax.random.uniform(key_rows, (TOKENS, 1), jnp.float32)
    column_scale = 10.0 ** columns
    return (0.1 * sample * row_scale * column_scale[None, :]).astype(jnp.bfloat16)


def draw_out_weight(key, part):
    key_noise = jax.random.fold_in(key, 21)
    key_signs = jax.random.fold_in(key, 22)
    key_levels = jax.random.fold_in(key, 23)
    key_flips = jax.random.fold_in(key, 24)
    row_count = HEADS * HEAD_DIM
    columns = jnp.arange(D, dtype=jnp.float32) / D
    fan_scale = row_count ** (-0.5)
    region = jnp.arange(D) * 4 // D
    row_signs = jax.random.rademacher(key_signs, (row_count, 4), jnp.float32)
    column_level = jax.random.uniform(key_levels, (D,), jnp.float32, 0.5, 1.5)
    column_level = column_level * jax.random.rademacher(key_flips, (D,), jnp.float32)
    shared = 1.5 * row_signs[:, region] * column_level[None, :]
    sample = jax.random.truncated_normal(key_noise, -4.0, 4.0, (row_count, D), jnp.float32)
    column_scale = 10.0 ** columns / 4.6
    return ((sample + shared) * fan_scale * column_scale[None, :]).astype(jnp.bfloat16)


def spread_heads(head_scale, head_count):
    return jnp.broadcast_to(head_scale[:, None], (head_count, HEAD_DIM)).reshape(head_count * HEAD_DIM)


def draw_query_weight(key, part):
    key_noise = jax.random.fold_in(key, 31)
    key_heads = jax.random.fold_in(key, 32)
    sample = jax.random.truncated_normal(key_noise, -4.0, 4.0, (D, HEADS * HEAD_DIM), jnp.float32)
    head_scale = 2.0 * 3.0 ** jax.random.uniform(key_heads, (HEADS,), jnp.float32)
    column_scale = spread_heads(head_scale, HEADS)
    return (sample * D ** (-0.5) * column_scale[None, :]).astype(jnp.bfloat16)


def draw_key_weight(key, part):
    key_noise = jax.random.fold_in(key, 41)
    key_order = jax.random.fold_in(key, 42)
    key_jitter = jax.random.fold_in(key, 43)
    sample = jax.random.truncated_normal(key_noise, -4.0, 4.0, (D, KV_HEADS * HEAD_DIM), jnp.float32)
    order = jax.random.permutation(key_order, KV_HEADS).astype(jnp.float32)
    level = (order + jax.random.uniform(key_jitter, (KV_HEADS,), jnp.float32)) / KV_HEADS
    head_scale = 6.0 ** level
    column_scale = spread_heads(head_scale, KV_HEADS)
    return (sample * D ** (-0.5) * column_scale[None, :]).astype(jnp.bfloat16)


def spiked(result, own_key, source, target, parts, factor):
    def block_of(axis_at):
        return (jnp.arange(result.shape[axis_at]) // (result.shape[axis_at] // parts)).reshape((-1,) + (1,) * (result.ndim - 1 - axis_at))

    near = jax.random.permutation(own_key, parts)[block_of(target)]
    far = (block_of(target) + parts // 2) % parts
    return jnp.where((block_of(source) == near) | (block_of(source) == far), factor * result, result)


def block_scale(own_key, dims, split, smallest, largest):
    gain, own = 1.0, jax.random.fold_in(own_key, 6)
    for dim, parts in split:
        heights = jnp.exp(jax.random.uniform(jax.random.fold_in(own, dim), (parts,), jnp.float32, smallest / len(split), largest / len(split)))
        gain = gain * jnp.repeat(heights, dims[dim] // parts).reshape([-1 if axis == dim else 1 for axis in range(len(dims))])
    return gain


def bell_draw(rng, dims, deviation, most, cuts=(), held_as=jnp.bfloat16):
    entries = jax.random.normal(rng, dims, jnp.float32) * deviation
    if len(cuts) > 0:
        entries = block_scale(rng, dims, cuts, -0.22, 0.18) * entries
    return jnp.clip(entries, min=-most, max=most).astype(held_as)


def heavy_noise(own_key, dims, width, reach, cuts, heavy, kind=jnp.bfloat16):
    array = width * jax.random.normal(own_key, dims, jnp.float32)
    if cuts:
        array = array * block_scale(own_key, dims, cuts, -0.22, 0.18)
    return jnp.clip(spiked(array, jax.random.fold_in(own_key, 3), *heavy), -reach, reach).astype(kind)


def setup_inputs(seed: int = 0) -> dict:
    arg_keys = jax.random.split(jax.random.key(seed), 12)
    return {
        "residual": draw_residual(jax.random.fold_in(arg_keys[11], 71), 0),
        "norm_gain": jnp.clip(1.0 + 0.15 * jax.random.normal(arg_keys[1], (D,), jnp.float32), 0.25, 1.75),
        "query_weight": draw_query_weight(jax.random.fold_in(arg_keys[11], 71), 0),
        "key_weight": draw_key_weight(jax.random.fold_in(arg_keys[11], 71), 0),
        "value_weight": bell_draw(arg_keys[4], (D, KV_HEADS * HEAD_DIM), D ** -0.5, 0.09375, ((0, 16), (1, 2))),
        "out_weight": draw_out_weight(jax.random.fold_in(arg_keys[11], 71), 0),
        "post_gain": jnp.clip(1.0 + 0.15 * jax.random.normal(arg_keys[6], (D,), jnp.float32), 0.25, 1.75),
        "encoder_weight": bell_draw(arg_keys[7], (D, LATENTS), D ** -0.5, 0.09375, ((1, 32),)),
        "encoder_bias": bell_draw(arg_keys[8], (LATENTS,), 0.5, 3.0, ((0, 32),), jnp.float32),
        "decoder_weight": heavy_noise(arg_keys[9], (LATENTS, D), LATENTS ** -0.5, 0.125, ((0, 32),), (0, 1, 32, 2.75)),
        "decoder_bias": bell_draw(arg_keys[10], (D,), 0.5, 3.0, (), jnp.float32),
    }


epsilon = 1e-06
softcap = 50.0
query_scale = 1.0 / 12.0
rope_base = 10000.0
smoothing = 0.1
penalty = 1.0
loss_weight = 0.0625

def rotate(matrix, positions):
    half_dim = matrix.shape[-1] // 2
    frequency = rope_base ** (-2.0 * jnp.arange(half_dim, dtype=jnp.float32) / matrix.shape[-1])
    angles = positions.astype(jnp.float32)[:, None] * frequency[None, :]
    cosine = jnp.cos(angles)[:, None, :]
    sine_part = jnp.sin(angles)[:, None, :]
    front_half = matrix[..., :half_dim]
    back_half = matrix[..., half_dim:]
    return jnp.concatenate([front_half * cosine - back_half * sine_part, back_half * cosine + front_half * sine_part], axis=-1)

def reference(residual, norm_gain, query_weight, key_weight, value_weight, out_weight, post_gain, encoder_weight, encoder_bias, decoder_weight, decoder_bias):
    residual_float = residual.astype(jnp.float32)
    scaled = (residual_float * norm_gain).astype(jnp.bfloat16)
    inverse = lax.rsqrt(lax.optimization_barrier(jnp.sum(residual_float * residual_float, axis=1)) / D + epsilon)
    query_raw = jnp.dot(scaled, query_weight, preferred_element_type=jnp.float32) * inverse[:, None]
    key_raw = jnp.dot(scaled, key_weight, preferred_element_type=jnp.float32) * inverse[:, None]
    value_raw = jnp.dot(scaled, value_weight, preferred_element_type=jnp.float32) * inverse[:, None]
    positions = jnp.arange(TOKENS).astype(jnp.int32)
    queries = rotate(query_raw.reshape(TOKENS, HEADS, HEAD_DIM), positions).astype(jnp.bfloat16)
    keys = rotate(key_raw.reshape(TOKENS, KV_HEADS, HEAD_DIM), positions).astype(jnp.bfloat16)
    values = value_raw.reshape(TOKENS, KV_HEADS, HEAD_DIM).astype(jnp.bfloat16)
    grouped = queries.astype(jnp.float32).reshape(TOKENS, KV_HEADS, HEADS // KV_HEADS, HEAD_DIM)
    scores = jnp.einsum('rkgd,skd->kgrs', grouped, keys.astype(jnp.float32)) * query_scale
    capped = softcap * jnp.tanh(scores / softcap)
    allowed = positions[:, None] >= positions[None, :]
    weights = jnp.where(allowed, jnp.exp(capped), jnp.float32(0.0))
    denominator = lax.optimization_barrier(jnp.sum(weights, axis=3))
    weights_low = lax.optimization_barrier(weights.astype(jnp.bfloat16)).astype(jnp.float32)
    numerator = jnp.einsum('kgrs,skd->rkgd', weights_low, values.astype(jnp.float32)).reshape(TOKENS, HEADS, HEAD_DIM)
    totals = jnp.transpose(denominator, (2, 0, 1)).reshape(TOKENS, HEADS)
    attended = (numerator / totals[:, :, None]).astype(jnp.bfloat16).reshape(TOKENS, HEADS * HEAD_DIM)
    head_out = jnp.dot(attended, out_weight, preferred_element_type=jnp.float32)
    normed = head_out * lax.rsqrt(lax.optimization_barrier(jnp.sum(head_out * head_out, axis=1)) / D + epsilon)[:, None] * post_gain
    hidden = (residual_float + normed).astype(jnp.bfloat16)
    preact = jnp.dot(hidden, encoder_weight, preferred_element_type=jnp.float32) + encoder_bias
    active = smoothing * jax.nn.softplus(preact / smoothing)
    active_low = active.astype(jnp.bfloat16)
    gate_slope = jax.nn.sigmoid(preact / smoothing)
    rebuilt = jnp.dot(active_low, decoder_weight, preferred_element_type=jnp.float32)
    error_low = (rebuilt + decoder_bias - hidden.astype(jnp.float32)).astype(jnp.bfloat16)
    decoder_norms = jnp.sqrt(lax.optimization_barrier(jnp.sum(jnp.square(decoder_weight.astype(jnp.float32)), axis=1)) + epsilon)
    feedback = jnp.dot(error_low, decoder_weight.T, preferred_element_type=jnp.float32)
    grad_active = loss_weight * (2.0 * feedback + penalty * decoder_norms)
    grad_preact = grad_active * gate_slope
    encoder_grad = jnp.dot(hidden.T, grad_preact.astype(jnp.bfloat16), preferred_element_type=jnp.float32).astype(jnp.bfloat16)
    encoder_bias_grad = lax.optimization_barrier(jnp.sum(grad_preact, axis=0))
    outer_sum = jnp.dot(active_low.T, error_low, preferred_element_type=jnp.float32)
    activity = lax.optimization_barrier(jnp.sum(active, axis=0))
    decoder_grad = (loss_weight * (2.0 * outer_sum + penalty * (activity / decoder_norms)[:, None] * decoder_weight.astype(jnp.float32))).astype(jnp.bfloat16)
    return (encoder_grad, encoder_bias_grad, decoder_grad)
```

```python
import functools

import jax
import jax.numpy as jnp
from jax import lax
from jax.experimental import pallas as pl
from jax.experimental.pallas import tpu as pltpu
from jax.sharding import PartitionSpec as P

HEAD_DIM = 128
CHUNKS = 2

epsilon = 1e-06
softcap = 50.0
query_scale = 1.0 / 12.0
rope_base = 10000.0
smoothing = 0.1
penalty = 1.0
loss_weight = 0.0625

bf16 = jnp.bfloat16
f32 = jnp.float32
AXES = ("dp", "mp")


class Ladder:
    def __init__(self, dp, mp):
        self.dp, self.mp = dp, mp
        dp_bits, mp_bits = dp.bit_length() - 1, mp.bit_length() - 1
        assert dp == 1 << dp_bits and mp == 1 << mp_bits
        self.near = [("dp", k) for k in range(min(2, dp_bits))]
        self.far = [("dp", k) for k in range(dp_bits - 1, len(self.near) - 1, -1)]
        self.cores = [("mp", k) for k in range(mp_bits - 1, -1, -1)]

    def place(self, step, m):
        axis, k = step
        if axis == "dp" and k < 2 and len(self.near) == 2 and m & 1:
            k = 1 - k
        return axis, k

    def pairs(self, step):
        result = []
        for d in range(self.dp):
            for m in range(self.mp):
                axis, k = self.place(step, m)
                peer = (d ^ (1 << k), m) if axis == "dp" else (d, m ^ (1 << k))
                result.append((d * self.mp + m, peer[0] * self.mp + peer[1]))
        return result

    def static_bit(self, step, d, m):
        axis, k = self.place(step, m)
        return ((d if axis == "dp" else m) >> k) & 1

    def bit(self, step):
        d, m = lax.axis_index("dp"), lax.axis_index("mp")
        axis, k = step
        if axis == "mp":
            return (m >> k) & 1
        if k < 2 and len(self.near) == 2:
            k = jnp.where(m & 1 == 1, 1 - k, k)
        return (d >> k) & 1

    def swap(self, value, step):
        return lax.ppermute(value, AXES, self.pairs(step))

    def scatter(self, value, steps, wire):
        for step in steps:
            half = value.shape[0] // 2
            up = self.bit(step) == 1
            low, high = value[:half], value[half:]
            got = self.swap(jnp.where(up, low, high).astype(wire), step)
            value = jnp.where(up, high, low) + got.astype(f32)
        return value

    def gather(self, value, steps):
        for step in reversed(steps):
            got = self.swap(value, step)
            up = self.bit(step) == 1
            value = jnp.concatenate([jnp.where(up, got, value), jnp.where(up, value, got)], axis=0)
        return value

    def order(self, steps):
        where = {}
        for d in range(self.dp):
            for m in range(self.mp):
                p = 0
                for step in steps:
                    p = 2 * p + self.static_bit(step, d, m)
                where[p] = d * self.mp + m
        return [where[p] for p in range(self.dp * self.mp)]

    def position(self, steps):
        p = 0
        for step in steps:
            p = 2 * p + self.bit(step)
        return p


def attention_kernel(start, heads, own_ref, got_ref, inv_ref, cos_ref, sin_ref, oldk_ref, oldv_ref, out_ref, k_ref, v_ref):
    width = own_ref.shape[1]
    half = HEAD_DIM // 2
    inverse = inv_ref[...]
    cosine, sine = cos_ref[...], sin_ref[...]

    def rows(first, count):
        return (own_ref[pl.ds(first, count), :] + got_ref[pl.ds(first, count), :].astype(f32)) * inverse

    def rotated(first):
        front, back = rows(first, half), rows(first + half, half)
        return jnp.concatenate([front * cosine - back * sine, back * cosine + front * sine], axis=0).astype(bf16)

    base = heads * HEAD_DIM
    k_ref[pl.ds(0, HEAD_DIM), pl.ds(start, width)] = rotated(base)
    v_ref[pl.ds(0, HEAD_DIM), pl.ds(start, width)] = rows(base + HEAD_DIM, HEAD_DIM).astype(bf16)
    if start:
        k_ref[:, pl.ds(0, start)] = oldk_ref[...]
        v_ref[:, pl.ds(0, start)] = oldv_ref[...]
    keys, values = k_ref[...], v_ref[...]
    span = start + width
    allowed = lax.broadcasted_iota(jnp.int32, (span, width), 0) <= lax.broadcasted_iota(jnp.int32, (span, width), 1) + start
    for h in range(heads):
        query = rotated(h * HEAD_DIM)
        score = lax.dot_general(keys, query, (((0,), (0,)), ((), ())), preferred_element_type=f32) * query_scale
        capped = softcap * jnp.tanh(score / softcap)
        weights = jnp.where(allowed, jnp.exp(capped), 0.0)
        total = jnp.sum(weights, axis=0, keepdims=True)
        mixed = jnp.dot(values, weights.astype(bf16), preferred_element_type=f32)
        out_ref[pl.ds(h * HEAD_DIM, HEAD_DIM), :] = (mixed / total).astype(bf16)


def attend(start, heads, own, got, inverse, cosine, sine, oldk, oldv):
    width = own.shape[1]
    span = start + width
    return pl.pallas_call(
        functools.partial(attention_kernel, start, heads),
        out_shape=(
            jax.ShapeDtypeStruct((heads * HEAD_DIM, width), bf16),
            jax.ShapeDtypeStruct((HEAD_DIM, span), bf16),
            jax.ShapeDtypeStruct((HEAD_DIM, span), bf16),
        ),
        cost_estimate=pl.CostEstimate(
            flops=4 * heads * HEAD_DIM * span * width, bytes_accessed=8 * own.size, transcendentals=2 * heads * span * width
        ),
    )(own, got, inverse, cosine, sine, oldk, oldv)


def on_device(ladder, residual, norm_gain, query_weight, key_weight, value_weight, out_weight, post_gain,
              encoder_weight, encoder_bias, decoder_weight, decoder_bias):
    tokens = residual.shape[0]
    model_width = decoder_weight.shape[1]
    latents = decoder_weight.shape[0]
    groups = key_weight.shape[1] // HEAD_DIM
    heads = query_weight.shape[1] // key_weight.shape[1]
    width = tokens // CHUNKS
    cuts = [slice(c * width, (c + 1) * width) for c in range(CHUNKS)]

    near, far, cores = ladder.near, ladder.far, ladder.cores
    dp_steps = near + far
    all_steps = cores + dp_steps
    group_bits = groups.bit_length() - 1
    assert groups == 1 << group_bits and group_bits <= len(dp_steps)
    group_steps, copy_steps = dp_steps[:group_bits], dp_steps[group_bits:]

    residual_t = residual.T
    residual_float = residual_t.astype(f32)
    scaled = (residual_float * norm_gain[:, None]).astype(bf16)
    pieces = []
    for g in range(groups):
        pieces += [
            query_weight[:, g * heads * HEAD_DIM : (g + 1) * heads * HEAD_DIM],
            key_weight[:, g * HEAD_DIM : (g + 1) * HEAD_DIM],
            value_weight[:, g * HEAD_DIM : (g + 1) * HEAD_DIM],
        ]
    stacked = jnp.concatenate(pieces, axis=1)
    projected = lax.dot_general(stacked, scaled, (((0,), (0,)), ((), ())), preferred_element_type=f32)

    mine = residual_t
    for step in cores:
        half = mine.shape[0] // 2
        mine = jnp.where(ladder.bit(step) == 1, mine[half:], mine[:half])
    order = ladder.order(all_steps)
    block = model_width // len(order)
    back = [order.index(i) for i in range(len(order))]

    def reordered(value, places):
        return jnp.concatenate([value[p * block : (p + 1) * block] for p in places], axis=0)

    encoder_g = reordered(encoder_weight, order)
    gain_all = lax.all_gather(post_gain, "dp", axis=0, tiled=True)
    gain_g = reordered(gain_all, order)

    half_dim = HEAD_DIM // 2
    frequency = rope_base ** (-2.0 * jnp.arange(half_dim, dtype=f32) / HEAD_DIM)
    angles = frequency[:, None] * jnp.arange(tokens).astype(f32)[None, :]
    cosine, sine = jnp.cos(angles), jnp.sin(angles)

    norms = jnp.sqrt(jnp.sum(jnp.square(decoder_weight.astype(f32)), axis=1) + epsilon)
    slot = ladder.position(all_steps) * block

    oldk = oldv = jnp.zeros((HEAD_DIM, width), bf16)
    hiddens, actives, slopes, errors = [], [], [], []
    activity = 0.0
    for c, cut in enumerate(cuts):
        residual_g = ladder.gather(mine[:, cut], all_steps)
        square_sum = jnp.sum(jnp.square(residual_g.astype(f32)), axis=0, keepdims=True)
        inverse = lax.rsqrt(square_sum / model_width + epsilon)

        part = ladder.scatter(projected[:, cut], group_steps, bf16)
        for step in copy_steps[:-1]:
            part = part + ladder.swap(part.astype(bf16), step).astype(f32)
        got = ladder.swap(part.astype(bf16), copy_steps[-1])
        attended, oldk, oldv = attend(
            c * width, heads, part, got, inverse, cosine[:, cut], sine[:, cut], oldk, oldv
        )
        attended = ladder.gather(attended, group_steps)
        head_part = lax.dot_general(out_weight, attended, (((0,), (0,)), ((), ())), preferred_element_type=f32)
        head_mine = ladder.scatter(head_part, cores, f32)
        head_g = ladder.gather(head_mine.astype(bf16), all_steps).astype(f32)
        head_squares = jnp.sum(jnp.square(head_g), axis=0, keepdims=True)
        head_inverse = lax.rsqrt(head_squares / model_width + epsilon)
        hidden_g = (residual_g.astype(f32) + head_g * head_inverse * gain_g[:, None]).astype(bf16)
        preact = (
            lax.dot_general(encoder_g, hidden_g, (((0,), (0,)), ((), ())), preferred_element_type=f32)
            + encoder_bias[:, None]
        )
        active = smoothing * jax.nn.softplus(preact / smoothing)
        active_low = active.astype(bf16)
        slopes.append(jax.nn.sigmoid(preact / smoothing))
        activity = activity + jnp.sum(active, axis=1)
        rebuilt_part = lax.dot_general(
            decoder_weight, active_low, (((0,), (0,)), ((), ())), preferred_element_type=f32
        )
        rebuilt = ladder.scatter(rebuilt_part, all_steps, bf16)
        hidden = reordered(hidden_g, back)
        error = (
            rebuilt
            + lax.dynamic_slice_in_dim(decoder_bias, slot, block)[:, None]
            - lax.dynamic_slice_in_dim(hidden, slot, block, axis=0).astype(f32)
        ).astype(bf16)
        errors.append(ladder.gather(error, all_steps))
        hiddens.append(hidden)
        actives.append(active_low)

    hidden = jnp.concatenate(hiddens, axis=1)
    active_low = jnp.concatenate(actives, axis=1)
    slope = jnp.concatenate(slopes, axis=1)
    error_low = jnp.concatenate(errors, axis=1)
    feedback = jnp.dot(decoder_weight, error_low, preferred_element_type=f32)
    grad_preact = loss_weight * (2.0 * feedback + penalty * norms[:, None]) * slope
    encoder_grad = lax.dot_general(
        hidden, grad_preact.astype(bf16), (((1,), (1,)), ((), ())), preferred_element_type=f32
    ).astype(bf16)
    encoder_bias_grad = jnp.sum(grad_preact, axis=1)
    outer_sum = lax.dot_general(active_low, error_low, (((1,), (1,)), ((), ())), preferred_element_type=f32)
    decoder_grad = (
        loss_weight * (2.0 * outer_sum + penalty * (activity / norms)[:, None] * decoder_weight.astype(f32))
    ).astype(bf16)
    return encoder_grad, encoder_bias_grad, decoder_grad


def solution(mesh):
    ladder = Ladder(mesh.shape["dp"], mesh.shape["mp"])
    placed = (
        P(None, "dp"),
        P("dp"),
        P("dp", "mp"),
        P("dp", "mp"),
        P("dp", "mp"),
        P("mp", "dp"),
        P("dp"),
        P(None, ("dp", "mp")),
        P(("dp", "mp")),
        P(("dp", "mp"), None),
        P(),
    )
    return jax.shard_map(
        functools.partial(on_device, ladder),
        mesh=mesh,
        in_specs=placed,
        out_specs=(P(None, ("dp", "mp")), P(("dp", "mp")), P(("dp", "mp"), None)),
        check_vma=False,
    )
```

```python
import functools

import jax
import jax.numpy as jnp
from jax import lax
from jax.experimental import pallas as pl
from jax.experimental.pallas import tpu as pltpu
from jax.sharding import PartitionSpec as P

HEAD_DIM = 128
CHUNKS = 2
EXTRA = 16

epsilon = 1e-06
softcap = 50.0
query_scale = 1.0 / 12.0
rope_base = 10000.0
smoothing = 0.1
penalty = 1.0
loss_weight = 0.0625

bf16 = jnp.bfloat16
f32 = jnp.float32
AXES = ("dp", "mp")


class Ladder:
    def __init__(self, dp, mp):
        self.dp, self.mp = dp, mp
        dp_bits, mp_bits = dp.bit_length() - 1, mp.bit_length() - 1
        assert dp == 1 << dp_bits and mp == 1 << mp_bits
        self.dp_bits = dp_bits
        self.cores = [(("mp", k), ("mp", k)) for k in range(mp_bits - 1, -1, -1)]

    def route(self, even, odd):
        if self.dp_bits < len(even):
            even = odd = tuple(range(self.dp_bits))
        rest = tuple(range(len(even), self.dp_bits))
        return [(("dp", j), ("dp", k)) for j, k in zip(even + rest, odd + rest)]

    def pairs(self, step):
        result = []
        for d in range(self.dp):
            for m in range(self.mp):
                axis, k = step[m & 1]
                peer = (d ^ (1 << k), m) if axis == "dp" else (d, m ^ (1 << k))
                result.append((d * self.mp + m, peer[0] * self.mp + peer[1]))
        return result

    def static_bit(self, step, d, m):
        axis, k = step[m & 1]
        return ((d if axis == "dp" else m) >> k) & 1

    def bit(self, step):
        d, m = lax.axis_index("dp"), lax.axis_index("mp")
        (axis, even), (_, odd) = step
        value = d if axis == "dp" else m
        if even == odd:
            return (value >> even) & 1
        return jnp.where(m & 1 == 0, (value >> even) & 1, (value >> odd) & 1)

    def swap(self, value, step):
        return lax.ppermute(value, AXES, self.pairs(step))

    def scatter(self, value, steps, wire):
        for step in steps:
            half = value.shape[0] // 2
            up = self.bit(step) == 1
            low, high = value[:half], value[half:]
            got = self.swap(jnp.where(up, low, high).astype(wire), step)
            value = jnp.where(up, high, low) + got.astype(f32)
        return value

    def gather(self, value, steps):
        for step in reversed(steps):
            got = self.swap(value, step)
            up = self.bit(step) == 1
            value = jnp.concatenate([jnp.where(up, got, value), jnp.where(up, value, got)], axis=0)
        return value

    def quarters(self, value, core, steps):
        own = self.gather(value, steps[1:])
        far = self.swap(own, steps[0])
        return own, far, self.swap(own, core), self.swap(far, core)

    def order(self, steps):
        where = {}
        for d in range(self.dp):
            for m in range(self.mp):
                p = 0
                for step in steps:
                    p = 2 * p + self.static_bit(step, d, m)
                where[p] = d * self.mp + m
        return [where[p] for p in range(self.dp * self.mp)]

    def position(self, steps):
        p = 0
        for step in steps:
            p = 2 * p + self.bit(step)
        return p

    def piece(self, core, step, k):
        up = self.bit(core)
        if k < 2:
            near = self.bit(step)
            return up, near if k == 0 else 1 - near
        d, m = lax.axis_index("dp"), lax.axis_index("mp") ^ (1 << core[0][1])
        (axis, even), (_, odd) = step
        value = d if axis == "dp" else m
        near = jnp.where(m & 1 == 0, (value >> even) & 1, (value >> odd) & 1)
        return 1 - up, near if k == 2 else 1 - near


VMEM = pl.BlockSpec(memory_space=pltpu.VMEM)
SMALL = pltpu.CompilerParams(vmem_limit_bytes=6 << 20)


def aligned(index, size):
    return pl.ds(pl.multiple_of(index * size, size), size)


def square_rows(total, ref, first):
    high = total.astype(bf16).astype(f32)
    place = lax.broadcasted_iota(jnp.int32, (EXTRA, total.shape[1]), 0)
    rows = jnp.where(place == 0, high, jnp.where(place == 1, total - high, 0.0))
    ref[pl.ds(first, EXTRA), :] = rows.astype(bf16)


def column(ref, width):
    return jnp.broadcast_to(ref[...][None, :], (width, ref.shape[0])).T


def project_kernel(ladder, step, groups, heads, chunks, residual_ref, gain_ref, *refs):
    weights, outs = refs[:3], refs[3 : 3 + 3 * chunks]
    query_ref, key_ref, value_ref = refs[-4:-1]
    copies = [pltpu.make_async_copy(w, r, refs[-1].at[i]) for i, (w, r) in enumerate(zip(weights, refs[-4:-1]))]
    for copy in copies:
        copy.start()
    up = ladder.bit(step)
    tokens = residual_ref.shape[1]
    width = tokens // chunks
    wide = heads * HEAD_DIM
    residual = residual_ref[...].astype(f32)
    scaled = (residual * column(gain_ref, tokens)).astype(bf16)
    square = jnp.sum(residual * residual, axis=0, keepdims=True)
    for copy in copies:
        copy.wait()
    sends, keeps, squares = outs[:chunks], outs[chunks : 2 * chunks], outs[2 * chunks :]
    half = groups // 2

    def times(weight):
        return lax.dot_general(weight, scaled, (((0,), (0,)), ((), ())), preferred_element_type=f32)

    for refs, side in ((sends, 1 - up), (keeps, up)):
        for j in range(half):
            g = side * half + j
            first = j * (wide + 2 * HEAD_DIM)
            for weight, size in ((query_ref, wide), (key_ref, HEAD_DIM), (value_ref, HEAD_DIM)):
                value = times(weight[:, aligned(g, size)])
                for c, ref in enumerate(refs):
                    ref[pl.ds(first, size), :] = value[:, c * width : (c + 1) * width].astype(ref.dtype)
                first += size
    for c in range(chunks):
        part = square[:, c * width : (c + 1) * width]
        squares[c][...] = part
        square_rows(part, sends[c], half * (wide + 2 * HEAD_DIM))


def project(ladder, step, groups, heads, residual, gain, query, key, value):
    width = residual.shape[1] // CHUNKS
    rows = groups // 2 * (heads + 2) * HEAD_DIM
    shapes = (
        [jax.ShapeDtypeStruct((rows + EXTRA, width), bf16)] * CHUNKS
        + [jax.ShapeDtypeStruct((rows, width), f32)] * CHUNKS
        + [jax.ShapeDtypeStruct((1, width), f32)] * CHUNKS
    )
    outs = pl.pallas_call(
        functools.partial(project_kernel, ladder, step, groups, heads, CHUNKS),
        out_shape=shapes,
        in_specs=[VMEM] * 2 + [pl.BlockSpec(memory_space=pltpu.HBM)] * 3,
        scratch_shapes=[
            pltpu.VMEM(query.shape, bf16),
            pltpu.VMEM(key.shape, bf16),
            pltpu.VMEM(value.shape, bf16),
            pltpu.SemaphoreType.DMA((3,)),
        ],
        compiler_params=pltpu.CompilerParams(vmem_limit_bytes=10 << 20),
        cost_estimate=pl.CostEstimate(
            flops=4 * rows * residual.size, bytes_accessed=2 * (query.size + key.size + value.size), transcendentals=0
        ),
    )(residual, gain, query, key, value)
    return outs[:CHUNKS], outs[CHUNKS : 2 * CHUNKS], outs[2 * CHUNKS :]


def step_kernel(ladder, step, halve, own_ref, got_ref, square_ref, send_ref, keep_ref, total_ref):
    rows, kept = own_ref.shape[0], keep_ref.shape[0]
    total = square_ref[...] + jnp.sum(got_ref[pl.ds(rows, EXTRA), :].astype(f32), axis=0, keepdims=True)
    total_ref[...] = total
    square_rows(total, send_ref, kept)
    if halve:
        up = ladder.bit(step)
        here, there = aligned(up, kept), aligned(1 - up, kept)
        send_ref[pl.ds(0, kept), :] = (own_ref[there, :] + got_ref[there, :].astype(f32)).astype(bf16)
        keep_ref[...] = own_ref[here, :] + got_ref[here, :].astype(f32)
    else:
        value = own_ref[...] + got_ref[pl.ds(0, rows), :].astype(f32)
        send_ref[pl.ds(0, kept), :] = value.astype(bf16)
        keep_ref[...] = value


def advance(ladder, step, halve, own, got, square):
    rows, width = own.shape
    kept = rows // 2 if halve else rows
    return pl.pallas_call(
        functools.partial(step_kernel, ladder, step, halve),
        out_shape=(
            jax.ShapeDtypeStruct((kept + EXTRA, width), bf16),
            jax.ShapeDtypeStruct((kept, width), f32),
            jax.ShapeDtypeStruct((1, width), f32),
        ),
        in_specs=[VMEM] * 3,
        compiler_params=SMALL,
        cost_estimate=pl.CostEstimate(flops=2 * own.size, bytes_accessed=12 * own.size, transcendentals=0),
    )(own, got, square)


def attention_kernel(start, heads, model_width, own_ref, got_ref, square_ref, cos_ref, sin_ref, *refs):
    oldk_ref, oldv_ref = refs[:2] if start else (None, None)
    out_ref, k_ref, v_ref = refs[-3:]
    width = own_ref.shape[1]
    half = HEAD_DIM // 2
    body = own_ref.shape[0]
    tail = jnp.sum(got_ref[pl.ds(body, EXTRA), :].astype(f32), axis=0, keepdims=True)
    inverse = lax.rsqrt((square_ref[...] + tail) / model_width + epsilon)
    lanes = pl.ds(start, width)
    cosine, sine = cos_ref[:, lanes], sin_ref[:, lanes]

    def rows(first, count):
        return (own_ref[pl.ds(first, count), :] + got_ref[pl.ds(first, count), :].astype(f32)) * inverse

    def rotated(first):
        front, back = rows(first, half), rows(first + half, half)
        return jnp.concatenate([front * cosine - back * sine, back * cosine + front * sine], axis=0).astype(bf16)

    base = heads * HEAD_DIM
    k_ref[:, pl.ds(start, width)] = rotated(base)
    v_ref[:, pl.ds(start, width)] = rows(base + HEAD_DIM, HEAD_DIM).astype(bf16)
    if start:
        k_ref[:, pl.ds(0, start)] = oldk_ref[...]
        v_ref[:, pl.ds(0, start)] = oldv_ref[...]
    keys, values = k_ref[...], v_ref[...]
    span = start + width
    allowed = lax.broadcasted_iota(jnp.int32, (span, width), 0) <= lax.broadcasted_iota(jnp.int32, (span, width), 1) + start
    for h in range(heads):
        query = rotated(h * HEAD_DIM)
        score = lax.dot_general(keys, query, (((0,), (0,)), ((), ())), preferred_element_type=f32) * query_scale
        capped = softcap * jnp.tanh(score / softcap)
        weights = jnp.where(allowed, jnp.exp(capped), 0.0)
        total = jnp.sum(weights, axis=0, keepdims=True)
        mixed = jnp.dot(values, weights.astype(bf16), preferred_element_type=f32)
        out_ref[pl.ds(h * HEAD_DIM, HEAD_DIM), :] = (mixed / total).astype(bf16)


def attend(start, heads, model_width, own, got, square, cosine, sine, *old):
    width = own.shape[1]
    span = start + width
    return pl.pallas_call(
        functools.partial(attention_kernel, start, heads, model_width),
        out_shape=(
            jax.ShapeDtypeStruct((heads * HEAD_DIM, width), bf16),
            jax.ShapeDtypeStruct((HEAD_DIM, span), bf16),
            jax.ShapeDtypeStruct((HEAD_DIM, span), bf16),
        ),
        compiler_params=SMALL,
        cost_estimate=pl.CostEstimate(
            flops=4 * heads * HEAD_DIM * span * width, bytes_accessed=8 * own.size, transcendentals=2 * heads * span * width
        ),
    )(own, got, square, cosine, sine, *old)


def out_kernel(ladder, near, core, own_ref, got_ref, weight_ref, send_ref, keep_ref):
    rows, columns = send_ref.shape[0], own_ref.shape[0]
    order, up = ladder.bit(near), ladder.bit(core)
    here, there = aligned(order, columns), aligned(1 - order, columns)
    for ref, half in ((send_ref, 1 - up), (keep_ref, up)):
        part = aligned(half, rows)
        ref[...] = jnp.dot(weight_ref[part, here], own_ref[...], preferred_element_type=f32) + jnp.dot(
            weight_ref[part, there], got_ref[...], preferred_element_type=f32
        )


def project_out(ladder, near, core, own, got, weight):
    shape = jax.ShapeDtypeStruct((weight.shape[0] // 2, own.shape[1]), f32)
    return pl.pallas_call(
        functools.partial(out_kernel, ladder, near, core),
        out_shape=(shape, shape),
        in_specs=[VMEM] * 3,
        compiler_params=SMALL,
        cost_estimate=pl.CostEstimate(
            flops=2 * weight.size * own.shape[1], bytes_accessed=2 * weight.size, transcendentals=0
        ),
    )(own, got, weight)


def pack_kernel(ladder, core, keep_ref, got_ref, gain_ref, packed_ref):
    head = keep_ref[...] + got_ref[...]
    rows, width = head.shape
    gain = column(gain_ref, width)
    gain = jnp.where(ladder.bit(core) == 1, gain[rows:], gain[:rows])
    packed_ref[pl.ds(0, rows), :] = (head * gain).astype(bf16)
    square_rows(jnp.sum(head * head, axis=0, keepdims=True), packed_ref, rows)


def pack(ladder, core, keep, got, gain):
    return pl.pallas_call(
        functools.partial(pack_kernel, ladder, core),
        out_shape=jax.ShapeDtypeStruct((keep.shape[0] + EXTRA, keep.shape[1]), bf16),
        in_specs=[VMEM] * 3,
        compiler_params=SMALL,
        cost_estimate=pl.CostEstimate(flops=4 * keep.size, bytes_accessed=10 * keep.size, transcendentals=0),
    )(keep, got, gain)


def targets(ladder, core, step, places, block, count, k):
    if not places:
        return [pl.ds((k * count + p) * block, block) for p in range(count)]
    side, near = ladder.piece(core, step, k)
    result = []
    for p in range(count):
        a, b, c, d = (places[q * count + p] for q in range(4))
        place = jnp.where(side == 0, jnp.where(near == 0, a, b), jnp.where(near == 0, c, d))
        result.append(aligned(place, block))
    return result


def assemble_kernel(ladder, core, step, places, block, *refs):
    out_ref = refs[4]
    count = refs[0].shape[0] // block
    for k in range(4):
        for p, target in enumerate(targets(ladder, core, step, places, block, count, k)):
            out_ref[target, :] = refs[k][pl.ds(p * block, block), :]


def assemble(ladder, core, step, places, block, pieces):
    rows, width = pieces[0].shape
    return pl.pallas_call(
        functools.partial(assemble_kernel, ladder, core, step, places, block),
        out_shape=jax.ShapeDtypeStruct((4 * rows, width), bf16),
        in_specs=[VMEM] * 4,
        compiler_params=pltpu.CompilerParams(vmem_limit_bytes=8 << 20),
        cost_estimate=pl.CostEstimate(flops=0, bytes_accessed=16 * rows * width, transcendentals=0),
    )(*pieces)


def hidden_kernel(ladder, core, step, places, first, block, model_width, *refs):
    pieces = refs[:4]
    residual_ref, enc_any, bias_ref, dec_any = refs[4:8]
    hidden_ref, low_ref, slope_ref, activity_ref, send_ref, keep_ref = refs[8:14]
    enc_ref, dec_ref, sems = refs[14:]
    load_enc = pltpu.make_async_copy(enc_any, enc_ref, sems.at[0])
    load_dec = pltpu.make_async_copy(dec_any, dec_ref, sems.at[1])
    load_enc.start()
    load_dec.start()
    width = pieces[0].shape[1]
    stride = block + EXTRA
    count = pieces[0].shape[0] // stride
    lanes = pl.ds(first, width)
    tail = jnp.zeros((EXTRA, width), f32)
    for ref in pieces:
        for p in range(count):
            tail = tail + ref[pl.ds(p * stride + block, EXTRA), :].astype(f32)
    inverse = lax.rsqrt(jnp.sum(tail, axis=0, keepdims=True) / model_width + epsilon)
    for k, ref in enumerate(pieces):
        for p, target in enumerate(targets(ladder, core, step, places, block, count, k)):
            value = residual_ref[target, lanes].astype(f32) + ref[pl.ds(p * stride, block), :].astype(f32) * inverse
            hidden_ref[target, :] = value.astype(bf16)
    load_enc.wait()
    preact = lax.dot_general(enc_ref[...], hidden_ref[...], (((0,), (0,)), ((), ())), preferred_element_type=f32)
    scaled = (preact + column(bias_ref, width)) / smoothing
    active = smoothing * (jnp.maximum(scaled, 0.0) + jnp.log1p(jnp.exp(-jnp.abs(scaled))))
    low = active.astype(bf16)
    low_ref[...] = low
    slope_ref[...] = jax.nn.sigmoid(scaled)
    activity_ref[...] = jnp.sum(active, axis=1, keepdims=True)
    half = send_ref.shape[0]
    up = ladder.bit(core)
    tile = half // 9
    load_dec.wait()
    for ref, side in ((send_ref, 1 - up), (keep_ref, up)):
        for t in range(9):
            rows = pl.ds(pl.multiple_of(side * half + t * tile, tile), tile)
            value = lax.dot_general(dec_ref[:, rows], low, (((0,), (0,)), ((), ())), preferred_element_type=f32)
            ref[pl.ds(t * tile, tile), :] = value.astype(ref.dtype)


def encode(ladder, core, step, places, first, block, pieces, residual, encoder, bias, decoder):
    width = pieces[0].shape[1]
    model_width, latents = encoder.shape
    any_space = pl.BlockSpec(memory_space=pltpu.HBM)
    return pl.pallas_call(
        functools.partial(hidden_kernel, ladder, core, step, places, first, block, model_width),
        out_shape=(
            jax.ShapeDtypeStruct((model_width, width), bf16),
            jax.ShapeDtypeStruct((latents, width), bf16),
            jax.ShapeDtypeStruct((latents, width), f32),
            jax.ShapeDtypeStruct((latents, 1), f32),
            jax.ShapeDtypeStruct((model_width // 2, width), bf16),
            jax.ShapeDtypeStruct((model_width // 2, width), f32),
        ),
        in_specs=[VMEM] * 5 + [any_space, VMEM, any_space],
        scratch_shapes=[
            pltpu.VMEM(encoder.shape, bf16),
            pltpu.VMEM(decoder.shape, bf16),
            pltpu.SemaphoreType.DMA((2,)),
        ],
        compiler_params=pltpu.CompilerParams(vmem_limit_bytes=(5 * encoder.size + (8 << 20))),
        cost_estimate=pl.CostEstimate(
            flops=4 * encoder.size * width, bytes_accessed=4 * encoder.size, transcendentals=4 * latents * width
        ),
    )(*pieces, residual, encoder, bias, decoder)


def final_kernel(ladder, core, steps, *refs):
    chunks = CHUNKS
    errors = [refs[4 * c : 4 * c + 4] for c in range(chunks)]
    refs = refs[4 * chunks :]
    hidden_any, low, slope, activity = (refs[i * chunks : (i + 1) * chunks] for i in range(4))
    dec_any, norm_ref, enc_out, bias_ref, dec_out = refs[4 * chunks : 4 * chunks + 5]
    hidden, dec_ref, error, enc_buf, dec_buf, in_sem, enc_sem, dec_sem = refs[4 * chunks + 5 :]
    width = hidden_any[0].shape[1]
    load_dec = pltpu.make_async_copy(dec_any, dec_ref, in_sem.at[0])
    load_dec.start()
    loads = []
    for c in range(chunks):
        place = hidden.at[:, pl.ds(c * width, width)]
        loads.append(pltpu.make_async_copy(hidden_any[c], place, in_sem.at[c + 1]))
        loads[-1].start()
    quarter = errors[0][0].shape[0]
    for c in range(chunks):
        for k in range(4):
            side, near = ladder.piece(core, steps[c], k)
            error[aligned(2 * side + near, quarter), pl.ds(c * width, width)] = errors[c][k][...]
    lows = jnp.concatenate([ref[...] for ref in low], axis=1)
    slopes = jnp.concatenate([ref[...] for ref in slope], axis=1)
    norms = column(norm_ref, 128)[:, :1]
    load_dec.wait()
    feedback = jnp.dot(dec_ref[...], error[...], preferred_element_type=f32)
    turned = (loss_weight * (2.0 * feedback + penalty * norms) * slopes).T
    bias_ref[...] = jnp.sum(turned, axis=0, keepdims=True)
    turned = turned.astype(bf16)
    copies = []

    def send(buf, out, index, sem):
        copies.append(pltpu.make_async_copy(buf.at[index], out.at[index], sem))
        copies[-1].start()

    for load in loads:
        load.wait()
    tile = hidden.shape[0] // 9
    for t in range(9):
        rows = pl.ds(t * tile, tile)
        enc_buf[rows, :] = jnp.dot(hidden[rows, :], turned, preferred_element_type=f32).astype(bf16)
        send(enc_buf, enc_out, (rows, slice(None)), enc_sem.at[t])
    ratio = loss_weight * penalty * sum(ref[...] for ref in activity) / norms
    for t in range(9):
        columns = pl.ds(t * tile, tile)
        outer = lax.dot_general(lows, error[columns, :], (((1,), (1,)), ((), ())), preferred_element_type=f32)
        dec_buf[:, columns] = (2.0 * loss_weight * outer + ratio * dec_ref[:, columns].astype(f32)).astype(bf16)
        send(dec_buf, dec_out, (slice(None), columns), dec_sem.at[t])
    for copy in copies:
        copy.wait()


def gradients(ladder, core, steps, errors, hidden, low, slope, activity, decoder, norms):
    latents, model_width = decoder.shape
    tokens = CHUNKS * hidden[0].shape[1]
    hbm = pl.BlockSpec(memory_space=pltpu.HBM)
    flat = [piece for pieces in errors for piece in pieces]
    return pl.pallas_call(
        functools.partial(final_kernel, ladder, core, steps),
        out_shape=(
            jax.ShapeDtypeStruct((model_width, latents), bf16),
            jax.ShapeDtypeStruct((1, latents), f32),
            jax.ShapeDtypeStruct((latents, model_width), bf16),
        ),
        in_specs=[VMEM] * len(flat) + [hbm] * CHUNKS + [VMEM] * (3 * CHUNKS) + [hbm, VMEM],
        out_specs=(hbm, VMEM, hbm),
        scratch_shapes=[
            pltpu.VMEM((model_width, tokens), bf16),
            pltpu.VMEM((latents, model_width), bf16),
            pltpu.VMEM((model_width, tokens), bf16),
            pltpu.VMEM((model_width, latents), bf16),
            pltpu.VMEM((latents, model_width), bf16),
            pltpu.SemaphoreType.DMA((1 + CHUNKS,)),
            pltpu.SemaphoreType.DMA((9,)),
            pltpu.SemaphoreType.DMA((9,)),
        ],
        compiler_params=pltpu.CompilerParams(
            vmem_limit_bytes=6 * decoder.size + 8 * model_width * tokens + (6 << 20)
        ),
        cost_estimate=pl.CostEstimate(
            flops=6 * decoder.size * tokens, bytes_accessed=12 * decoder.size, transcendentals=0
        ),
    )(*flat, *hidden, *low, *slope, *activity, decoder, norms)


def split_rows(value):
    high = lax.reduce_precision(value, 8, 7)
    rows = jnp.concatenate([high, value - high], axis=0).astype(bf16)
    return jnp.concatenate([rows, jnp.zeros((EXTRA - 2, value.shape[1]), bf16)], axis=0)


def on_device(ladder, residual, norm_gain, query_weight, key_weight, value_weight, out_weight, post_gain,
              encoder_weight, encoder_bias, decoder_weight, decoder_bias):
    tokens = residual.shape[0]
    model_width = decoder_weight.shape[1]
    groups = key_weight.shape[1] // HEAD_DIM
    heads = query_weight.shape[1] // key_weight.shape[1]
    width = tokens // CHUNKS
    cuts = [slice(c * width, (c + 1) * width) for c in range(CHUNKS)]

    cores = ladder.cores
    dp_steps = ladder.route((0, 1, 2), (1, 0, 2))
    routes = [ladder.route((0, 1, 2), (1, 2, 0)), ladder.route((2, 0, 1), (1, 0, 2))]
    group_bits = groups.bit_length() - 1
    assert groups == 1 << group_bits and group_bits <= len(dp_steps)
    group_steps, copy_steps = dp_steps[:group_bits], dp_steps[group_bits:]

    residual_t = residual.T
    core = cores[0]
    core_bit = ladder.bit(core)
    paired = len(cores) == 1 and residual_t.shape[0] % 32 == 0 and group_bits >= 1

    mine, gain = residual_t, post_gain[:, None]
    for step in cores:
        half = mine.shape[0] // 2
        up = ladder.bit(step) == 1
        mine = jnp.where(up, mine[half:], mine[:half])
        gain = jnp.where(up, gain[half:], gain[:half])
    block = mine.shape[0]

    def canonical(pieces, steps, stride):
        own, far, own_peer, far_peer = pieces
        value = []
        for k, (a, b) in ((0, (own, far)), (2, (own_peer, far_peer))):
            _, near = ladder.piece(core, steps[0], k)
            value.append(jnp.concatenate([jnp.where(near == 1, b, a), jnp.where(near == 1, a, b)], axis=0))
        own, got = value
        value = jnp.concatenate([jnp.where(core_bit == 1, got, own), jnp.where(core_bit == 1, own, got)], axis=0)
        order = ladder.order(cores[:1] + steps)
        return jnp.concatenate(
            [value[p * stride : p * stride + block] for p in (order.index(i) for i in range(len(order)))], axis=0
        )

    def cut_four(value):
        quarter = value.shape[0] // 4
        return [value[k * quarter : (k + 1) * quarter] for k in range(4)]

    steps = cores[1:] + routes[0]
    residual_own = ladder.gather(mine, steps[1:])
    residual_far = ladder.swap(residual_own, steps[0])
    half_dim = HEAD_DIM // 2
    frequency = rope_base ** (-2.0 * jnp.arange(half_dim, dtype=f32) / HEAD_DIM)
    angles = frequency[:, None] * jnp.arange(tokens).astype(f32)[None, :]
    cosine, sine = jnp.cos(angles), jnp.sin(angles)

    out_t = out_weight.T
    norms = jnp.sqrt(jnp.sum(jnp.square(decoder_weight.astype(f32)), axis=1) + epsilon)

    if paired:
        sends, keeps, squares = project(
            ladder, dp_steps[0], groups, heads, residual_t, norm_gain, query_weight, key_weight, value_weight
        )
    else:
        residual_float = residual_t.astype(f32)
        scaled = (residual_float * norm_gain[:, None]).astype(bf16)
        square = jnp.sum(residual_float * residual_float, axis=0, keepdims=True)
        pieces = []
        for g in range(groups):
            pieces += [
                query_weight[:, g * heads * HEAD_DIM : (g + 1) * heads * HEAD_DIM],
                key_weight[:, g * HEAD_DIM : (g + 1) * HEAD_DIM],
                value_weight[:, g * HEAD_DIM : (g + 1) * HEAD_DIM],
            ]
        stacked = jnp.concatenate(pieces, axis=1)
        projected = lax.dot_general(stacked, scaled, (((0,), (0,)), ((), ())), preferred_element_type=f32)
        sends, keeps, squares = [], [], []
        for cut in cuts:
            send = keep = projected[:, cut]
            if group_bits:
                half = send.shape[0] // 2
                up = ladder.bit(dp_steps[0]) == 1
                send, keep = jnp.where(up, keep[:half], keep[half:]), jnp.where(up, keep[half:], keep[:half])
            sends.append(jnp.concatenate([send.astype(bf16), split_rows(square[:, cut])], axis=0))
            keeps.append(keep)
            squares.append(square[:, cut])

    old = ()
    attendeds = []
    errors, nears, hiddens, lows, slopes, activities = [], [], [], [], [], []
    for c in range(CHUNKS):
        send, part, square = sends[c], keeps[c], squares[c]
        for i, step in enumerate(dp_steps):
            got = ladder.swap(send, step)
            if i < len(dp_steps) - 1:
                send, part, square = advance(ladder, dp_steps[i + 1], i + 1 < group_bits, part, got, square)
        attended, *old = attend(c * width, heads, model_width, part, got, square, cosine, sine, *old)
        attendeds.append(attended)

    residuals = (residual_own, residual_far, ladder.swap(residual_own, core), ladder.swap(residual_far, core))
    if paired:
        residual_all = assemble(ladder, core, steps[0], ladder.order(cores + routes[0]), block, residuals)
    else:
        residual_all = canonical(residuals, steps, block)

    for c, attended in enumerate(attendeds):
        if paired:
            attended = ladder.gather(attended, group_steps[1:])
            got = ladder.swap(attended, group_steps[0])
            send, keep = project_out(ladder, group_steps[0], core, attended, got, out_t)
            packed = pack(ladder, core, keep, ladder.swap(send, core), post_gain)
        else:
            attended = ladder.gather(attended, group_steps)
            head = ladder.scatter(jnp.dot(out_t, attended, preferred_element_type=f32), cores, f32)
            packed = jnp.concatenate(
                [(head * gain).astype(bf16), split_rows(jnp.sum(head * head, axis=0, keepdims=True))], axis=0
            )
        steps = routes[c % len(routes)]
        pieces = ladder.quarters(packed, core, cores[1:] + steps)
        near = (cores[1:] + steps)[0]
        kernel_block, places = block, ladder.order(cores + steps)
        if not paired:
            stride = block + EXTRA
            tails = sum(
                v[p * stride + block : (p + 1) * stride].astype(f32)
                for v in pieces
                for p in range(v.shape[0] // stride)
            )
            tails = split_rows(jnp.sum(tails, axis=0, keepdims=True))
            whole = cut_four(canonical(pieces, cores[1:] + steps, stride))
            pieces = [
                jnp.concatenate([v, tails if k == 0 else jnp.zeros_like(tails)], axis=0) for k, v in enumerate(whole)
            ]
            kernel_block, places = model_width // 4, ()
        if c == CHUNKS - 1:
            last, norms = lax.optimization_barrier((pieces[-1], norms))
            pieces = (*pieces[:-1], last)
        hidden, low, slope, activity, send, part = encode(
            ladder, core, near, places, c * width, kernel_block, pieces, residual_all,
            encoder_weight, encoder_bias, decoder_weight,
        )
        part = part + ladder.swap(send, core).astype(f32)
        rebuilt = ladder.scatter(part, cores[1:] + steps, bf16)
        slot = ladder.position(cores + steps) * block
        bias_mine = lax.dynamic_slice_in_dim(decoder_bias, slot, block)[:, None]
        error = (rebuilt + bias_mine - lax.dynamic_slice_in_dim(hidden, slot, block, axis=0).astype(f32)).astype(bf16)
        errors.append(ladder.quarters(error, core, cores[1:] + steps))
        nears.append(near)
        hiddens.append(hidden)
        lows.append(low)
        slopes.append(slope)
        activities.append(activity)

    encoder_grad, encoder_bias_grad, decoder_grad = gradients(
        ladder, core, nears, errors, hiddens, lows, slopes, activities, decoder_weight, norms
    )
    return encoder_grad, encoder_bias_grad[0], decoder_grad


def solution(mesh):
    ladder = Ladder(mesh.shape["dp"], mesh.shape["mp"])
    placed = (
        P(None, "dp"),
        P("dp"),
        P("dp", "mp"),
        P("dp", "mp"),
        P("dp", "mp"),
        P("mp", "dp"),
        P("dp"),
        P(None, ("dp", "mp")),
        P(("dp", "mp")),
        P(("dp", "mp"), None),
        P(),
    )
    return jax.shard_map(
        functools.partial(on_device, ladder),
        mesh=mesh,
        in_specs=placed,
        out_specs=(P(None, ("dp", "mp")), P(("dp", "mp")), P(("dp", "mp"), None)),
        check_vma=False,
    )
```

```python
import functools

import jax
import jax.numpy as jnp
from jax import lax
from jax.experimental import pallas as pl
from jax.experimental.pallas import tpu as pltpu
from jax.sharding import PartitionSpec as P

HEAD_DIM = 128
CHUNKS = 2
EXTRA = 16

epsilon = 1e-06
softcap = 50.0
query_scale = 1.0 / 12.0
rope_base = 10000.0
smoothing = 0.1
penalty = 1.0
loss_weight = 0.0625

bf16 = jnp.bfloat16
f32 = jnp.float32
AXES = ("dp", "mp")


class Ladder:
    def __init__(self, dp, mp):
        self.dp, self.mp = dp, mp
        dp_bits, mp_bits = dp.bit_length() - 1, mp.bit_length() - 1
        assert dp == 1 << dp_bits and mp == 1 << mp_bits
        self.dp_bits = dp_bits
        self.cores = [(("mp", k), ("mp", k)) for k in range(mp_bits - 1, -1, -1)]

    def route(self, even, odd):
        if self.dp_bits < len(even):
            even = odd = tuple(range(self.dp_bits))
        rest = tuple(range(len(even), self.dp_bits))
        return [(("dp", j), ("dp", k)) for j, k in zip(even + rest, odd + rest)]

    def pairs(self, step):
        result = []
        for d in range(self.dp):
            for m in range(self.mp):
                axis, k = step[m & 1]
                peer = (d ^ (1 << k), m) if axis == "dp" else (d, m ^ (1 << k))
                result.append((d * self.mp + m, peer[0] * self.mp + peer[1]))
        return result

    def static_bit(self, step, d, m):
        axis, k = step[m & 1]
        return ((d if axis == "dp" else m) >> k) & 1

    def bit(self, step):
        d, m = lax.axis_index("dp"), lax.axis_index("mp")
        (axis, even), (_, odd) = step
        value = d if axis == "dp" else m
        if even == odd:
            return (value >> even) & 1
        return jnp.where(m & 1 == 0, (value >> even) & 1, (value >> odd) & 1)

    def swap(self, value, step):
        return lax.ppermute(value, AXES, self.pairs(step))

    def scatter(self, value, steps, wire):
        for step in steps:
            half = value.shape[0] // 2
            up = self.bit(step) == 1
            low, high = value[:half], value[half:]
            got = self.swap(jnp.where(up, low, high).astype(wire), step)
            value = jnp.where(up, high, low) + got.astype(f32)
        return value

    def gather(self, value, steps):
        for step in reversed(steps):
            got = self.swap(value, step)
            up = self.bit(step) == 1
            value = jnp.concatenate([jnp.where(up, got, value), jnp.where(up, value, got)], axis=0)
        return value

    def quarters(self, value, core, steps):
        own = self.gather(value, steps[1:])
        far = self.swap(own, steps[0])
        return own, far, self.swap(own, core), self.swap(far, core)

    def order(self, steps):
        where = {}
        for d in range(self.dp):
            for m in range(self.mp):
                p = 0
                for step in steps:
                    p = 2 * p + self.static_bit(step, d, m)
                where[p] = d * self.mp + m
        return [where[p] for p in range(self.dp * self.mp)]

    def position(self, steps):
        p = 0
        for step in steps:
            p = 2 * p + self.bit(step)
        return p

    def piece(self, core, step, k):
        up = self.bit(core)
        if k < 2:
            near = self.bit(step)
            return up, near if k == 0 else 1 - near
        d, m = lax.axis_index("dp"), lax.axis_index("mp") ^ (1 << core[0][1])
        (axis, even), (_, odd) = step
        value = d if axis == "dp" else m
        near = jnp.where(m & 1 == 0, (value >> even) & 1, (value >> odd) & 1)
        return 1 - up, near if k == 2 else 1 - near


VMEM = pl.BlockSpec(memory_space=pltpu.VMEM)


def in_hbm(value):
    return pltpu.with_memory_space_constraint(value, pltpu.HBM)


SMALL = pltpu.CompilerParams(vmem_limit_bytes=6 << 20)


def aligned(index, size):
    return pl.ds(pl.multiple_of(index * size, size), size)


def square_rows(total, ref, first):
    high = total.astype(bf16).astype(f32)
    place = lax.broadcasted_iota(jnp.int32, (EXTRA, total.shape[1]), 0)
    rows = jnp.where(place == 0, high, jnp.where(place == 1, total - high, 0.0))
    ref[pl.ds(first, EXTRA), :] = rows.astype(bf16)


def column(ref, width):
    return jnp.broadcast_to(ref[...][None, :], (width, ref.shape[0])).T


def project_kernel(ladder, step, groups, heads, chunks, residual_ref, gain_ref, *refs):
    weights, outs = refs[:3], refs[3 : 3 + 3 * chunks]
    query_ref, key_ref, value_ref = refs[-4:-1]
    copies = [pltpu.make_async_copy(w, r, refs[-1].at[i]) for i, (w, r) in enumerate(zip(weights, refs[-4:-1]))]
    for copy in copies:
        copy.start()
    up = ladder.bit(step)
    tokens = residual_ref.shape[1]
    width = tokens // chunks
    wide = heads * HEAD_DIM
    residual = residual_ref[...].astype(f32)
    scaled = (residual * column(gain_ref, tokens)).astype(bf16)
    square = jnp.sum(residual * residual, axis=0, keepdims=True)
    for copy in copies:
        copy.wait()
    sends, keeps, squares = outs[:chunks], outs[chunks : 2 * chunks], outs[2 * chunks :]
    half = groups // 2

    def times(weight):
        return lax.dot_general(weight, scaled, (((0,), (0,)), ((), ())), preferred_element_type=f32)

    for refs, side in ((sends, 1 - up), (keeps, up)):
        for j in range(half):
            g = side * half + j
            first = j * (wide + 2 * HEAD_DIM)
            for weight, size in ((query_ref, wide), (key_ref, HEAD_DIM), (value_ref, HEAD_DIM)):
                value = times(weight[:, aligned(g, size)])
                for c, ref in enumerate(refs):
                    ref[pl.ds(first, size), :] = value[:, c * width : (c + 1) * width].astype(ref.dtype)
                first += size
    for c in range(chunks):
        part = square[:, c * width : (c + 1) * width]
        squares[c][...] = part
        square_rows(part, sends[c], half * (wide + 2 * HEAD_DIM))


def project(ladder, step, groups, heads, residual, gain, query, key, value):
    width = residual.shape[1] // CHUNKS
    rows = groups // 2 * (heads + 2) * HEAD_DIM
    shapes = (
        [jax.ShapeDtypeStruct((rows + EXTRA, width), bf16)] * CHUNKS
        + [jax.ShapeDtypeStruct((rows, width), f32)] * CHUNKS
        + [jax.ShapeDtypeStruct((1, width), f32)] * CHUNKS
    )
    outs = pl.pallas_call(
        functools.partial(project_kernel, ladder, step, groups, heads, CHUNKS),
        out_shape=shapes,
        in_specs=[VMEM] * 2 + [pl.BlockSpec(memory_space=pltpu.HBM)] * 3,
        scratch_shapes=[
            pltpu.VMEM(query.shape, bf16),
            pltpu.VMEM(key.shape, bf16),
            pltpu.VMEM(value.shape, bf16),
            pltpu.SemaphoreType.DMA((3,)),
        ],
        compiler_params=pltpu.CompilerParams(vmem_limit_bytes=10 << 20),
        cost_estimate=pl.CostEstimate(
            flops=4 * rows * residual.size, bytes_accessed=2 * (query.size + key.size + value.size), transcendentals=0
        ),
    )(residual, gain, in_hbm(query), in_hbm(key), in_hbm(value))
    return list(outs[:CHUNKS]), outs[CHUNKS : 2 * CHUNKS], outs[2 * CHUNKS :]


def step_kernel(ladder, step, halve, own_ref, got_ref, square_ref, send_ref, keep_ref, total_ref):
    rows, kept = own_ref.shape[0], keep_ref.shape[0]
    total = square_ref[...] + jnp.sum(got_ref[pl.ds(rows, EXTRA), :].astype(f32), axis=0, keepdims=True)
    total_ref[...] = total
    square_rows(total, send_ref, kept)
    if halve:
        up = ladder.bit(step)
        here, there = aligned(up, kept), aligned(1 - up, kept)
        send_ref[pl.ds(0, kept), :] = (own_ref[there, :] + got_ref[there, :].astype(f32)).astype(bf16)
        keep_ref[...] = own_ref[here, :] + got_ref[here, :].astype(f32)
    else:
        value = own_ref[...] + got_ref[pl.ds(0, rows), :].astype(f32)
        send_ref[pl.ds(0, kept), :] = value.astype(bf16)
        keep_ref[...] = value


def advance(ladder, step, halve, own, got, square):
    rows, width = own.shape
    kept = rows // 2 if halve else rows
    return pl.pallas_call(
        functools.partial(step_kernel, ladder, step, halve),
        out_shape=(
            jax.ShapeDtypeStruct((kept + EXTRA, width), bf16),
            jax.ShapeDtypeStruct((kept, width), f32),
            jax.ShapeDtypeStruct((1, width), f32),
        ),
        in_specs=[VMEM] * 3,
        compiler_params=SMALL,
        cost_estimate=pl.CostEstimate(flops=2 * own.size, bytes_accessed=12 * own.size, transcendentals=0),
    )(own, got, square)


def attention_kernel(start, heads, model_width, own_ref, got_ref, square_ref, cos_ref, sin_ref, *refs):
    oldk_ref, oldv_ref = refs[:2] if start else (None, None)
    out_ref, k_ref, v_ref = refs[-3:]
    width = own_ref.shape[1]
    half = HEAD_DIM // 2
    body = own_ref.shape[0]
    tail = jnp.sum(got_ref[pl.ds(body, EXTRA), :].astype(f32), axis=0, keepdims=True)
    inverse = lax.rsqrt((square_ref[...] + tail) / model_width + epsilon)
    lanes = pl.ds(start, width)
    cosine, sine = cos_ref[:, lanes], sin_ref[:, lanes]

    def rows(first, count):
        return (own_ref[pl.ds(first, count), :] + got_ref[pl.ds(first, count), :].astype(f32)) * inverse

    def rotated(first):
        front, back = rows(first, half), rows(first + half, half)
        return jnp.concatenate([front * cosine - back * sine, back * cosine + front * sine], axis=0).astype(bf16)

    base = heads * HEAD_DIM
    k_ref[:, pl.ds(start, width)] = rotated(base)
    v_ref[:, pl.ds(start, width)] = rows(base + HEAD_DIM, HEAD_DIM).astype(bf16)
    if start:
        k_ref[:, pl.ds(0, start)] = oldk_ref[...]
        v_ref[:, pl.ds(0, start)] = oldv_ref[...]
    keys, values = k_ref[...], v_ref[...]
    span = start + width
    allowed = lax.broadcasted_iota(jnp.int32, (span, width), 0) <= lax.broadcasted_iota(jnp.int32, (span, width), 1) + start
    for h in range(heads):
        query = rotated(h * HEAD_DIM)
        score = lax.dot_general(keys, query, (((0,), (0,)), ((), ())), preferred_element_type=f32) * query_scale
        capped = softcap * jnp.tanh(score / softcap)
        weights = jnp.where(allowed, jnp.exp(capped), 0.0)
        total = jnp.sum(weights, axis=0, keepdims=True)
        mixed = jnp.dot(values, weights.astype(bf16), preferred_element_type=f32)
        out_ref[pl.ds(h * HEAD_DIM, HEAD_DIM), :] = (mixed / total).astype(bf16)


def attend(start, heads, model_width, own, got, square, cosine, sine, *old):
    width = own.shape[1]
    span = start + width
    return pl.pallas_call(
        functools.partial(attention_kernel, start, heads, model_width),
        out_shape=(
            jax.ShapeDtypeStruct((heads * HEAD_DIM, width), bf16),
            jax.ShapeDtypeStruct((HEAD_DIM, span), bf16),
            jax.ShapeDtypeStruct((HEAD_DIM, span), bf16),
        ),
        compiler_params=SMALL,
        cost_estimate=pl.CostEstimate(
            flops=4 * heads * HEAD_DIM * span * width, bytes_accessed=8 * own.size, transcendentals=2 * heads * span * width
        ),
    )(own, got, square, cosine, sine, *old)


def out_kernel(ladder, near, core, own_ref, got_ref, weight_ref, send_ref, keep_ref):
    rows, columns = send_ref.shape[0], own_ref.shape[0]
    order, up = ladder.bit(near), ladder.bit(core)
    here, there = aligned(order, columns), aligned(1 - order, columns)
    for ref, half in ((send_ref, 1 - up), (keep_ref, up)):
        part = aligned(half, rows)
        ref[...] = jnp.dot(weight_ref[part, here], own_ref[...], preferred_element_type=f32) + jnp.dot(
            weight_ref[part, there], got_ref[...], preferred_element_type=f32
        )


def project_out(ladder, near, core, own, got, weight):
    shape = jax.ShapeDtypeStruct((weight.shape[0] // 2, own.shape[1]), f32)
    return pl.pallas_call(
        functools.partial(out_kernel, ladder, near, core),
        out_shape=(shape, shape),
        in_specs=[VMEM] * 3,
        compiler_params=SMALL,
        cost_estimate=pl.CostEstimate(
            flops=2 * weight.size * own.shape[1], bytes_accessed=2 * weight.size, transcendentals=0
        ),
    )(own, got, weight)


def pack_kernel(ladder, core, keep_ref, got_ref, gain_ref, packed_ref):
    head = keep_ref[...] + got_ref[...]
    rows, width = head.shape
    gain = column(gain_ref, width)
    gain = jnp.where(ladder.bit(core) == 1, gain[rows:], gain[:rows])
    packed_ref[pl.ds(0, rows), :] = (head * gain).astype(bf16)
    square_rows(jnp.sum(head * head, axis=0, keepdims=True), packed_ref, rows)


def pack(ladder, core, keep, got, gain):
    return pl.pallas_call(
        functools.partial(pack_kernel, ladder, core),
        out_shape=jax.ShapeDtypeStruct((keep.shape[0] + EXTRA, keep.shape[1]), bf16),
        in_specs=[VMEM] * 3,
        compiler_params=SMALL,
        cost_estimate=pl.CostEstimate(flops=4 * keep.size, bytes_accessed=10 * keep.size, transcendentals=0),
    )(keep, got, gain)


def targets(ladder, core, step, places, block, count, k):
    if not places:
        return [pl.ds((k * count + p) * block, block) for p in range(count)]
    side, near = ladder.piece(core, step, k)
    result = []
    for p in range(count):
        a, b, c, d = (places[q * count + p] for q in range(4))
        place = jnp.where(side == 0, jnp.where(near == 0, a, b), jnp.where(near == 0, c, d))
        result.append(aligned(place, block))
    return result


def assemble_kernel(ladder, core, step, places, block, *refs):
    count = refs[0].shape[0] // block
    width = refs[4].shape[1]
    for k in range(4):
        for p, target in enumerate(targets(ladder, core, step, places, block, count, k)):
            value = refs[k][pl.ds(p * block, block), :]
            for c, out_ref in enumerate(refs[4:]):
                out_ref[target, :] = value[:, c * width : (c + 1) * width]


def assemble(ladder, core, step, places, block, pieces):
    rows, width = pieces[0].shape
    return pl.pallas_call(
        functools.partial(assemble_kernel, ladder, core, step, places, block),
        out_shape=[jax.ShapeDtypeStruct((4 * rows, width // CHUNKS), bf16)] * CHUNKS,
        in_specs=[VMEM] * 4,
        compiler_params=pltpu.CompilerParams(vmem_limit_bytes=8 << 20),
        cost_estimate=pl.CostEstimate(flops=0, bytes_accessed=16 * rows * width, transcendentals=0),
    )(*pieces)


def encode_kernel(ladder, core, steps, places, block, model_width, *refs):
    pieces = refs[:4]
    residual_ref, enc_any, bias_ref, offset_ref = refs[4:8]
    hidden_ref, low_ref, slope_ref, activity_ref, base_ref, hidden_buf, enc_ref, sems = refs[8:]
    load = pltpu.make_async_copy(enc_any, enc_ref, sems.at[1])
    load.start()
    width = pieces[0].shape[1]
    stride = block + EXTRA
    count = pieces[0].shape[0] // stride
    tail = jnp.zeros((EXTRA, width), f32)
    for ref in pieces:
        for p in range(count):
            tail = tail + ref[pl.ds(p * stride + block, EXTRA), :].astype(f32)
    inverse = lax.rsqrt(jnp.sum(tail, axis=0, keepdims=True) / model_width + epsilon)
    for k, ref in enumerate(pieces):
        for p, target in enumerate(targets(ladder, core, steps[1], places, block, count, k)):
            value = residual_ref[target, :].astype(f32) + ref[pl.ds(p * stride, block), :].astype(f32) * inverse
            hidden_buf[target, :] = value.astype(bf16)
    store = pltpu.make_async_copy(hidden_buf, hidden_ref, sems.at[0])
    store.start()
    if places:
        mine = hidden_buf[aligned(ladder.position(steps), block), :].astype(f32)
        base_ref[...] = column(offset_ref, width) - mine
    else:
        base_ref[...] = column(offset_ref, width)
    load.wait()
    preact = lax.dot_general(enc_ref[...], hidden_buf[...], (((0,), (0,)), ((), ())), preferred_element_type=f32)
    scaled = (preact + column(bias_ref, width)) / smoothing
    active = smoothing * (jnp.maximum(scaled, 0.0) + jnp.log1p(jnp.exp(-jnp.abs(scaled))))
    low_ref[...] = active.astype(bf16)
    slope_ref[...] = jax.nn.sigmoid(scaled)
    activity_ref[...] = jnp.sum(active, axis=1, keepdims=True)
    store.wait()


def encode(ladder, core, steps, places, block, pieces, residual, encoder, bias, offset):
    width = pieces[0].shape[1]
    model_width, latents = encoder.shape
    hbm = pl.BlockSpec(memory_space=pltpu.HBM)
    return pl.pallas_call(
        functools.partial(encode_kernel, ladder, core, steps, places, block, model_width),
        out_shape=(
            jax.ShapeDtypeStruct((model_width, width), bf16),
            jax.ShapeDtypeStruct((latents, width), bf16),
            jax.ShapeDtypeStruct((latents, width), f32),
            jax.ShapeDtypeStruct((latents, 1), f32),
            jax.ShapeDtypeStruct((offset.shape[0], width), f32),
        ),
        in_specs=[VMEM] * 5 + [hbm] + [VMEM] * 2,
        out_specs=[hbm] + [VMEM] * 4,
        scratch_shapes=[
            pltpu.VMEM((model_width, width), bf16),
            pltpu.VMEM(encoder.shape, bf16),
            pltpu.SemaphoreType.DMA((2,)),
        ],
        compiler_params=pltpu.CompilerParams(vmem_limit_bytes=2 * encoder.size + 8 * model_width * width + (4 << 20)),
        cost_estimate=pl.CostEstimate(
            flops=2 * encoder.size * width, bytes_accessed=2 * encoder.size, transcendentals=4 * latents * width
        ),
    )(*pieces, residual, in_hbm(encoder), bias, offset)


def decode_kernel(ladder, core, step, low_ref, peer_low_ref, dec_any, peer_dec_any, send_ref, keep_ref, buf, sems):
    up = ladder.bit(step)
    half = send_ref.shape[0]
    first = 2 * ladder.bit(core)
    loads = []
    for i, side in enumerate((1 - up, up)):
        for j, source in enumerate((dec_any, peer_dec_any)):
            loads.append(pltpu.make_async_copy(source.at[:, aligned(first + side, half)], buf.at[i, j], sems.at[2 * i + j]))
            loads[-1].start()
    lows = (low_ref[...], peer_low_ref[...])
    tile = half // 3
    for i, ref in enumerate((send_ref, keep_ref)):
        loads[2 * i].wait()
        loads[2 * i + 1].wait()
        for t in range(3):
            rows = pl.ds(t * tile, tile)
            value = sum(
                lax.dot_general(buf[i, j, :, rows], lows[j], (((0,), (0,)), ((), ())), preferred_element_type=f32)
                for j in range(2)
            )
            ref[rows, :] = value.astype(ref.dtype)


def decode(ladder, core, step, low, peer_low, decoder, peer_decoder):
    latents, width = low.shape
    half = decoder.shape[1] // 4
    hbm = pl.BlockSpec(memory_space=pltpu.HBM)
    return pl.pallas_call(
        functools.partial(decode_kernel, ladder, core, step),
        out_shape=(jax.ShapeDtypeStruct((half, width), bf16), jax.ShapeDtypeStruct((half, width), f32)),
        in_specs=[VMEM] * 2 + [hbm] * 2,
        scratch_shapes=[pltpu.VMEM((2, 2, latents, half), bf16), pltpu.SemaphoreType.DMA((4,))],
        compiler_params=pltpu.CompilerParams(vmem_limit_bytes=2 * decoder.size + 6 * half * width + (6 << 20)),
        cost_estimate=pl.CostEstimate(
            flops=4 * decoder.size * width, bytes_accessed=4 * decoder.size, transcendentals=0
        ),
    )(low, peer_low, in_hbm(decoder), in_hbm(peer_decoder))


def final_kernel(ladder, core, steps, *refs):
    chunks = CHUNKS
    errors = [refs[4 * c : 4 * c + 4] for c in range(chunks)]
    refs = refs[4 * chunks :]
    hidden_any, low, slope, activity = (refs[i * chunks : (i + 1) * chunks] for i in range(4))
    dec_any, norm_ref, enc_out, bias_ref, dec_out = refs[4 * chunks : 4 * chunks + 5]
    hidden, dec_ref, error, enc_buf, dec_buf, in_sem, enc_sem, dec_sem = refs[4 * chunks + 5 :]
    width = hidden_any[0].shape[1]
    load_dec = pltpu.make_async_copy(dec_any, dec_ref, in_sem.at[0])
    load_dec.start()
    loads = []
    for c in range(chunks):
        place = hidden.at[:, pl.ds(c * width, width)]
        loads.append(pltpu.make_async_copy(hidden_any[c], place, in_sem.at[c + 1]))
        loads[-1].start()
    quarter = errors[0][0].shape[0]
    for c in range(chunks):
        for k in range(4):
            side, near = ladder.piece(core, steps[c], k)
            error[aligned(2 * side + near, quarter), pl.ds(c * width, width)] = errors[c][k][...]
    lows = jnp.concatenate([ref[...] for ref in low], axis=1)
    slopes = jnp.concatenate([ref[...] for ref in slope], axis=1)
    norms = column(norm_ref, 128)[:, :1]
    load_dec.wait()
    feedback = jnp.dot(dec_ref[...], error[...], preferred_element_type=f32)
    turned = (loss_weight * (2.0 * feedback + penalty * norms) * slopes).T
    bias_ref[...] = jnp.sum(turned, axis=0, keepdims=True)
    turned = turned.astype(bf16)
    copies = []

    def send(buf, out, index, sem):
        copies.append(pltpu.make_async_copy(buf.at[index], out.at[index], sem))
        copies[-1].start()

    for load in loads:
        load.wait()
    tile = hidden.shape[0] // 9
    for t in range(9):
        rows = pl.ds(t * tile, tile)
        enc_buf[rows, :] = jnp.dot(hidden[rows, :], turned, preferred_element_type=f32).astype(bf16)
        send(enc_buf, enc_out, (rows, slice(None)), enc_sem.at[t])
    ratio = loss_weight * penalty * sum(ref[...] for ref in activity) / norms
    for t in range(9):
        columns = pl.ds(t * tile, tile)
        outer = lax.dot_general(lows, error[columns, :], (((1,), (1,)), ((), ())), preferred_element_type=f32)
        dec_buf[:, columns] = (2.0 * loss_weight * outer + ratio * dec_ref[:, columns].astype(f32)).astype(bf16)
        send(dec_buf, dec_out, (slice(None), columns), dec_sem.at[t])
    for copy in copies:
        copy.wait()


def gradients(ladder, core, steps, errors, hidden, low, slope, activity, decoder, norms):
    latents, model_width = decoder.shape
    tokens = CHUNKS * hidden[0].shape[1]
    hbm = pl.BlockSpec(memory_space=pltpu.HBM)
    flat = [piece for pieces in errors for piece in pieces]
    return pl.pallas_call(
        functools.partial(final_kernel, ladder, core, steps),
        out_shape=(
            jax.ShapeDtypeStruct((model_width, latents), bf16),
            jax.ShapeDtypeStruct((1, latents), f32),
            jax.ShapeDtypeStruct((latents, model_width), bf16),
        ),
        in_specs=[VMEM] * len(flat) + [hbm] * CHUNKS + [VMEM] * (3 * CHUNKS) + [hbm, VMEM],
        out_specs=(hbm, VMEM, hbm),
        scratch_shapes=[
            pltpu.VMEM((model_width, tokens), bf16),
            pltpu.VMEM((latents, model_width), bf16),
            pltpu.VMEM((model_width, tokens), bf16),
            pltpu.VMEM((model_width, latents), bf16),
            pltpu.VMEM((latents, model_width), bf16),
            pltpu.SemaphoreType.DMA((1 + CHUNKS,)),
            pltpu.SemaphoreType.DMA((9,)),
            pltpu.SemaphoreType.DMA((9,)),
        ],
        compiler_params=pltpu.CompilerParams(
            vmem_limit_bytes=6 * decoder.size + 8 * model_width * tokens + (6 << 20)
        ),
        cost_estimate=pl.CostEstimate(
            flops=6 * decoder.size * tokens, bytes_accessed=12 * decoder.size, transcendentals=0
        ),
    )(*flat, *hidden, *low, *slope, *activity, decoder, norms)


def split_rows(value):
    high = lax.reduce_precision(value, 8, 7)
    rows = jnp.concatenate([high, value - high], axis=0).astype(bf16)
    return jnp.concatenate([rows, jnp.zeros((EXTRA - 2, value.shape[1]), bf16)], axis=0)


def on_device(ladder, residual, norm_gain, query_weight, key_weight, value_weight, out_weight, post_gain,
              encoder_weight, encoder_bias, decoder_weight, decoder_bias):
    tokens = residual.shape[0]
    model_width = decoder_weight.shape[1]
    groups = key_weight.shape[1] // HEAD_DIM
    heads = query_weight.shape[1] // key_weight.shape[1]
    width = tokens // CHUNKS
    cuts = [slice(c * width, (c + 1) * width) for c in range(CHUNKS)]

    cores = ladder.cores
    dp_steps = ladder.route((0, 1, 2), (1, 0, 2))
    routes = [ladder.route((0, 1, 2), (1, 2, 0)), ladder.route((2, 0, 1), (1, 0, 2))]
    group_bits = groups.bit_length() - 1
    assert groups == 1 << group_bits and group_bits <= len(dp_steps)
    group_steps, copy_steps = dp_steps[:group_bits], dp_steps[group_bits:]

    residual_t = residual.T
    core = cores[0]
    core_bit = ladder.bit(core)
    paired = len(cores) == 1 and residual_t.shape[0] % 32 == 0 and group_bits >= 1

    mine, gain = residual_t, post_gain[:, None]
    for step in cores:
        half = mine.shape[0] // 2
        up = ladder.bit(step) == 1
        mine = jnp.where(up, mine[half:], mine[:half])
        gain = jnp.where(up, gain[half:], gain[:half])
    block = mine.shape[0]

    def canonical(pieces, steps, stride):
        own, far, own_peer, far_peer = pieces
        value = []
        for k, (a, b) in ((0, (own, far)), (2, (own_peer, far_peer))):
            _, near = ladder.piece(core, steps[0], k)
            value.append(jnp.concatenate([jnp.where(near == 1, b, a), jnp.where(near == 1, a, b)], axis=0))
        own, got = value
        value = jnp.concatenate([jnp.where(core_bit == 1, got, own), jnp.where(core_bit == 1, own, got)], axis=0)
        order = ladder.order(cores[:1] + steps)
        return jnp.concatenate(
            [value[p * stride : p * stride + block] for p in (order.index(i) for i in range(len(order)))], axis=0
        )

    def cut_four(value):
        quarter = value.shape[0] // 4
        return [value[k * quarter : (k + 1) * quarter] for k in range(4)]

    half_dim = HEAD_DIM // 2
    frequency = rope_base ** (-2.0 * jnp.arange(half_dim, dtype=f32) / HEAD_DIM)
    angles = frequency[:, None] * jnp.arange(tokens).astype(f32)[None, :]
    cosine, sine = jnp.cos(angles), jnp.sin(angles)

    out_t = out_weight.T
    decoder_peer = ladder.swap(decoder_weight, core)
    norms = jnp.sqrt(jnp.sum(jnp.square(decoder_weight.astype(f32)), axis=1) + epsilon)

    if paired:
        sends, keeps, squares = project(
            ladder, dp_steps[0], groups, heads, residual_t, norm_gain, query_weight, key_weight, value_weight
        )
    else:
        residual_float = residual_t.astype(f32)
        scaled = (residual_float * norm_gain[:, None]).astype(bf16)
        square = jnp.sum(residual_float * residual_float, axis=0, keepdims=True)
        pieces = []
        for g in range(groups):
            pieces += [
                query_weight[:, g * heads * HEAD_DIM : (g + 1) * heads * HEAD_DIM],
                key_weight[:, g * HEAD_DIM : (g + 1) * HEAD_DIM],
                value_weight[:, g * HEAD_DIM : (g + 1) * HEAD_DIM],
            ]
        stacked = jnp.concatenate(pieces, axis=1)
        projected = lax.dot_general(stacked, scaled, (((0,), (0,)), ((), ())), preferred_element_type=f32)
        sends, keeps, squares = [], [], []
        for cut in cuts:
            send = keep = projected[:, cut]
            if group_bits:
                half = send.shape[0] // 2
                up = ladder.bit(dp_steps[0]) == 1
                send, keep = jnp.where(up, keep[:half], keep[half:]), jnp.where(up, keep[half:], keep[:half])
            sends.append(jnp.concatenate([send.astype(bf16), split_rows(square[:, cut])], axis=0))
            keeps.append(keep)
            squares.append(square[:, cut])

    sends[0], mine = lax.optimization_barrier((sends[0], mine))
    steps = cores[1:] + routes[0]
    residual_own = ladder.gather(mine, steps[1:])
    residual_far = ladder.swap(residual_own, steps[0])
    old = ()
    attendeds = []
    errors, nears, hiddens, lows, slopes, activities = [], [], [], [], [], []
    for c in range(CHUNKS):
        send, part, square = sends[c], keeps[c], squares[c]
        for i, step in enumerate(dp_steps):
            got = ladder.swap(send, step)
            if i < len(dp_steps) - 1:
                send, part, square = advance(ladder, dp_steps[i + 1], i + 1 < group_bits, part, got, square)
        attended, *old = attend(c * width, heads, model_width, part, got, square, cosine, sine, *old)
        attendeds.append(attended)

    residuals = (residual_own, residual_far, ladder.swap(residual_own, core), ladder.swap(residual_far, core))
    if paired:
        residual_all = assemble(ladder, core, steps[0], ladder.order(cores + routes[0]), block, residuals)
    else:
        residual_all = canonical(residuals, steps, block)
        residual_all = [residual_all[:, cut] for cut in cuts]

    slots = [ladder.position(cores + routes[c % len(routes)]) * block for c in range(CHUNKS)]
    offsets = [lax.dynamic_slice_in_dim(decoder_bias, slot, block) for slot in slots]
    for c, attended in enumerate(attendeds):
        if paired:
            attended = ladder.gather(attended, group_steps[1:])
            got = ladder.swap(attended, group_steps[0])
            send, keep = project_out(ladder, group_steps[0], core, attended, got, out_t)
            packed = pack(ladder, core, keep, ladder.swap(send, core), post_gain)
        else:
            attended = ladder.gather(attended, group_steps)
            head = ladder.scatter(jnp.dot(out_t, attended, preferred_element_type=f32), cores, f32)
            packed = jnp.concatenate(
                [(head * gain).astype(bf16), split_rows(jnp.sum(head * head, axis=0, keepdims=True))], axis=0
            )
        steps = routes[c % len(routes)]
        path = cores[1:] + steps
        own = ladder.gather(packed, path[1:])
        if c == 1:
            own, norms, offsets, residual_all = lax.optimization_barrier((own, norms, offsets, residual_all))
        far = ladder.swap(own, path[0])
        pieces = own, far, ladder.swap(own, core), ladder.swap(far, core)
        near = (cores[1:] + steps)[0]
        kernel_block, places = block, ladder.order(cores + steps)
        if not paired:
            stride = block + EXTRA
            tails = sum(
                v[p * stride + block : (p + 1) * stride].astype(f32)
                for v in pieces
                for p in range(v.shape[0] // stride)
            )
            tails = split_rows(jnp.sum(tails, axis=0, keepdims=True))
            whole = cut_four(canonical(pieces, cores[1:] + steps, stride))
            pieces = [
                jnp.concatenate([v, tails if k == 0 else jnp.zeros_like(tails)], axis=0) for k, v in enumerate(whole)
            ]
            kernel_block, places = model_width // 4, ()
        slot, offset = slots[c], offsets[c]
        hidden, low, slope, activity, base = encode(
            ladder, core, cores + steps, places, kernel_block, pieces, residual_all[c], encoder_weight, encoder_bias, offset
        )
        if not paired:
            base = base - lax.dynamic_slice_in_dim(hidden, slot, block, axis=0).astype(f32)
        send, part = decode(ladder, core, path[0], low, ladder.swap(low, core), decoder_weight, decoder_peer)
        part = part + ladder.swap(send, path[0]).astype(f32)
        error = (ladder.scatter(part, path[1:], bf16) + base).astype(bf16)
        errors.append(ladder.quarters(error, core, cores[1:] + steps))
        nears.append(near)
        hiddens.append(hidden)
        lows.append(low)
        slopes.append(slope)
        activities.append(activity)

    encoder_grad, encoder_bias_grad, decoder_grad = gradients(
        ladder, core, nears, errors, hiddens, lows, slopes, activities, decoder_weight, norms
    )
    return encoder_grad, encoder_bias_grad[0], decoder_grad


def solution(mesh):
    ladder = Ladder(mesh.shape["dp"], mesh.shape["mp"])
    placed = (
        P(None, "dp"),
        P("dp"),
        P("dp", "mp"),
        P("dp", "mp"),
        P("dp", "mp"),
        P("mp", "dp"),
        P("dp"),
        P(None, ("dp", "mp")),
        P(("dp", "mp")),
        P(("dp", "mp"), None),
        P(),
    )
    return jax.shard_map(
        functools.partial(on_device, ladder),
        mesh=mesh,
        in_specs=placed,
        out_specs=(P(None, ("dp", "mp")), P(("dp", "mp")), P(("dp", "mp"), None)),
        check_vma=False,
    )
```

```python
import functools

import jax
import jax.numpy as jnp
from jax import lax
from jax.experimental import pallas as pl
from jax.experimental.pallas import tpu as pltpu
from jax.sharding import PartitionSpec as P

HEAD_DIM = 128
CHUNKS = 2
EXTRA = 16

epsilon = 1e-06
softcap = 50.0
query_scale = 1.0 / 12.0
rope_base = 10000.0
smoothing = 0.1
penalty = 1.0
loss_weight = 0.0625

bf16 = jnp.bfloat16
f32 = jnp.float32
AXES = ("dp", "mp")


class Ladder:
    def __init__(self, dp, mp):
        self.dp, self.mp = dp, mp
        dp_bits, mp_bits = dp.bit_length() - 1, mp.bit_length() - 1
        assert dp == 1 << dp_bits and mp == 1 << mp_bits
        self.dp_bits = dp_bits
        self.cores = [(("mp", k), ("mp", k)) for k in range(mp_bits - 1, -1, -1)]

    def route(self, even, odd):
        if self.dp_bits < len(even):
            even = odd = tuple(range(self.dp_bits))
        rest = tuple(range(len(even), self.dp_bits))
        return [(("dp", j), ("dp", k)) for j, k in zip(even + rest, odd + rest)]

    def pairs(self, step):
        result = []
        for d in range(self.dp):
            for m in range(self.mp):
                axis, k = step[m & 1]
                peer = (d ^ (1 << k), m) if axis == "dp" else (d, m ^ (1 << k))
                result.append((d * self.mp + m, peer[0] * self.mp + peer[1]))
        return result

    def static_bit(self, step, d, m):
        axis, k = step[m & 1]
        return ((d if axis == "dp" else m) >> k) & 1

    def bit(self, step):
        d, m = lax.axis_index("dp"), lax.axis_index("mp")
        (axis, even), (_, odd) = step
        value = d if axis == "dp" else m
        if even == odd:
            return (value >> even) & 1
        return jnp.where(m & 1 == 0, (value >> even) & 1, (value >> odd) & 1)

    def swap(self, value, step):
        return lax.ppermute(value, AXES, self.pairs(step))

    def scatter(self, value, steps, wire):
        for step in steps:
            half = value.shape[0] // 2
            up = self.bit(step) == 1
            low, high = value[:half], value[half:]
            got = self.swap(jnp.where(up, low, high).astype(wire), step)
            value = jnp.where(up, high, low) + got.astype(f32)
        return value

    def gather(self, value, steps):
        for step in reversed(steps):
            got = self.swap(value, step)
            up = self.bit(step) == 1
            value = jnp.concatenate([jnp.where(up, got, value), jnp.where(up, value, got)], axis=0)
        return value

    def quarters(self, value, core, steps):
        own = self.gather(value, steps[1:])
        far = self.swap(own, steps[0])
        return own, far, self.swap(own, core), self.swap(far, core)

    def order(self, steps):
        where = {}
        for d in range(self.dp):
            for m in range(self.mp):
                p = 0
                for step in steps:
                    p = 2 * p + self.static_bit(step, d, m)
                where[p] = d * self.mp + m
        return [where[p] for p in range(self.dp * self.mp)]

    def position(self, steps):
        p = 0
        for step in steps:
            p = 2 * p + self.bit(step)
        return p

    def piece(self, core, step, k):
        up = self.bit(core)
        if k < 2:
            near = self.bit(step)
            return up, near if k == 0 else 1 - near
        d, m = lax.axis_index("dp"), lax.axis_index("mp") ^ (1 << core[0][1])
        (axis, even), (_, odd) = step
        value = d if axis == "dp" else m
        near = jnp.where(m & 1 == 0, (value >> even) & 1, (value >> odd) & 1)
        return 1 - up, near if k == 2 else 1 - near


VMEM = pl.BlockSpec(memory_space=pltpu.VMEM)


def in_hbm(value):
    return pltpu.with_memory_space_constraint(value, pltpu.HBM)


def in_vmem(value):
    return pltpu.with_memory_space_constraint(value, pltpu.VMEM)


SMALL = pltpu.CompilerParams(vmem_limit_bytes=6 << 20)


def aligned(index, size):
    return pl.ds(pl.multiple_of(index * size, size), size)


def square_rows(total, ref, first):
    high = total.astype(bf16).astype(f32)
    place = lax.broadcasted_iota(jnp.int32, (EXTRA, total.shape[1]), 0)
    rows = jnp.where(place == 0, high, jnp.where(place == 1, total - high, 0.0))
    ref[pl.ds(first, EXTRA), :] = rows.astype(bf16)


def column(ref, width):
    return jnp.broadcast_to(ref[...][None, :], (width, ref.shape[0])).T


def project_kernel(ladder, step, groups, heads, chunks, residual_ref, gain_ref, *refs):
    weights, outs = refs[:3], refs[3 : 3 + 3 * chunks]
    query_ref, key_ref, value_ref = refs[-4:-1]
    copies = [pltpu.make_async_copy(w, r, refs[-1].at[i]) for i, (w, r) in enumerate(zip(weights, refs[-4:-1]))]
    for copy in copies:
        copy.start()
    up = ladder.bit(step)
    tokens = residual_ref.shape[1]
    width = tokens // chunks
    wide = heads * HEAD_DIM
    residual = residual_ref[...].astype(f32)
    scaled = (residual * column(gain_ref, tokens)).astype(bf16)
    square = jnp.sum(residual * residual, axis=0, keepdims=True)
    for copy in copies:
        copy.wait()
    sends, keeps, squares = outs[:chunks], outs[chunks : 2 * chunks], outs[2 * chunks :]
    half = groups // 2

    def times(weight):
        return lax.dot_general(weight, scaled, (((0,), (0,)), ((), ())), preferred_element_type=f32)

    for refs, side in ((sends, 1 - up), (keeps, up)):
        for j in range(half):
            g = side * half + j
            first = j * (wide + 2 * HEAD_DIM)
            for weight, size in ((query_ref, wide), (key_ref, HEAD_DIM), (value_ref, HEAD_DIM)):
                value = times(weight[:, aligned(g, size)])
                for c, ref in enumerate(refs):
                    ref[pl.ds(first, size), :] = value[:, c * width : (c + 1) * width].astype(ref.dtype)
                first += size
    for c in range(chunks):
        part = square[:, c * width : (c + 1) * width]
        squares[c][...] = part
        square_rows(part, sends[c], half * (wide + 2 * HEAD_DIM))


def project(ladder, step, groups, heads, residual, gain, query, key, value):
    width = residual.shape[1] // CHUNKS
    rows = groups // 2 * (heads + 2) * HEAD_DIM
    shapes = (
        [jax.ShapeDtypeStruct((rows + EXTRA, width), bf16)] * CHUNKS
        + [jax.ShapeDtypeStruct((rows, width), f32)] * CHUNKS
        + [jax.ShapeDtypeStruct((1, width), f32)] * CHUNKS
    )
    outs = pl.pallas_call(
        functools.partial(project_kernel, ladder, step, groups, heads, CHUNKS),
        out_shape=shapes,
        in_specs=[VMEM] * 2 + [pl.BlockSpec(memory_space=pltpu.HBM)] * 3,
        scratch_shapes=[
            pltpu.VMEM(query.shape, bf16),
            pltpu.VMEM(key.shape, bf16),
            pltpu.VMEM(value.shape, bf16),
            pltpu.SemaphoreType.DMA((3,)),
        ],
        compiler_params=pltpu.CompilerParams(vmem_limit_bytes=10 << 20),
        cost_estimate=pl.CostEstimate(
            flops=4 * rows * residual.size, bytes_accessed=2 * (query.size + key.size + value.size), transcendentals=0
        ),
    )(residual, gain, in_hbm(query), in_hbm(key), in_hbm(value))
    return list(outs[:CHUNKS]), outs[CHUNKS : 2 * CHUNKS], outs[2 * CHUNKS :]


def step_kernel(ladder, step, halve, own_ref, got_ref, square_ref, send_ref, keep_ref, total_ref):
    rows, kept = own_ref.shape[0], keep_ref.shape[0]
    total = square_ref[...] + jnp.sum(got_ref[pl.ds(rows, EXTRA), :].astype(f32), axis=0, keepdims=True)
    total_ref[...] = total
    square_rows(total, send_ref, kept)
    if halve:
        up = ladder.bit(step)
        here, there = aligned(up, kept), aligned(1 - up, kept)
        send_ref[pl.ds(0, kept), :] = (own_ref[there, :] + got_ref[there, :].astype(f32)).astype(bf16)
        keep_ref[...] = own_ref[here, :] + got_ref[here, :].astype(f32)
    else:
        value = own_ref[...] + got_ref[pl.ds(0, rows), :].astype(f32)
        send_ref[pl.ds(0, kept), :] = value.astype(bf16)
        keep_ref[...] = value


def advance(ladder, step, halve, own, got, square):
    rows, width = own.shape
    kept = rows // 2 if halve else rows
    return pl.pallas_call(
        functools.partial(step_kernel, ladder, step, halve),
        out_shape=(
            jax.ShapeDtypeStruct((kept + EXTRA, width), bf16),
            jax.ShapeDtypeStruct((kept, width), f32),
            jax.ShapeDtypeStruct((1, width), f32),
        ),
        in_specs=[VMEM] * 3,
        compiler_params=SMALL,
        cost_estimate=pl.CostEstimate(flops=2 * own.size, bytes_accessed=12 * own.size, transcendentals=0),
    )(own, got, square)


def attention_kernel(start, heads, model_width, own_ref, got_ref, square_ref, cos_ref, sin_ref, *refs):
    oldk_ref, oldv_ref = refs[:2] if start else (None, None)
    out_ref, k_ref, v_ref = refs[-3:]
    width = own_ref.shape[1]
    half = HEAD_DIM // 2
    body = own_ref.shape[0]
    tail = jnp.sum(got_ref[pl.ds(body, EXTRA), :].astype(f32), axis=0, keepdims=True)
    inverse = lax.rsqrt((square_ref[...] + tail) / model_width + epsilon)
    lanes = pl.ds(start, width)
    cosine, sine = cos_ref[:, lanes], sin_ref[:, lanes]

    def rows(first, count):
        return (own_ref[pl.ds(first, count), :] + got_ref[pl.ds(first, count), :].astype(f32)) * inverse

    def rotated(first):
        front, back = rows(first, half), rows(first + half, half)
        return jnp.concatenate([front * cosine - back * sine, back * cosine + front * sine], axis=0).astype(bf16)

    base = heads * HEAD_DIM
    k_ref[:, pl.ds(start, width)] = rotated(base)
    v_ref[:, pl.ds(start, width)] = rows(base + HEAD_DIM, HEAD_DIM).astype(bf16)
    if start:
        k_ref[:, pl.ds(0, start)] = oldk_ref[...]
        v_ref[:, pl.ds(0, start)] = oldv_ref[...]
    keys, values = k_ref[...], v_ref[...]
    span = start + width
    allowed = lax.broadcasted_iota(jnp.int32, (span, width), 0) <= lax.broadcasted_iota(jnp.int32, (span, width), 1) + start
    for h in range(heads):
        query = rotated(h * HEAD_DIM)
        score = lax.dot_general(keys, query, (((0,), (0,)), ((), ())), preferred_element_type=f32) * query_scale
        capped = softcap * jnp.tanh(score / softcap)
        weights = jnp.where(allowed, jnp.exp(capped), 0.0)
        total = jnp.sum(weights, axis=0, keepdims=True)
        mixed = jnp.dot(values, weights.astype(bf16), preferred_element_type=f32)
        out_ref[pl.ds(h * HEAD_DIM, HEAD_DIM), :] = (mixed / total).astype(bf16)


def attend(start, heads, model_width, own, got, square, cosine, sine, *old):
    width = own.shape[1]
    span = start + width
    return pl.pallas_call(
        functools.partial(attention_kernel, start, heads, model_width),
        out_shape=(
            jax.ShapeDtypeStruct((heads * HEAD_DIM, width), bf16),
            jax.ShapeDtypeStruct((HEAD_DIM, span), bf16),
            jax.ShapeDtypeStruct((HEAD_DIM, span), bf16),
        ),
        compiler_params=SMALL,
        cost_estimate=pl.CostEstimate(
            flops=4 * heads * HEAD_DIM * span * width, bytes_accessed=8 * own.size, transcendentals=2 * heads * span * width
        ),
    )(own, got, square, cosine, sine, *old)


def out_kernel(ladder, near, core, own_ref, got_ref, weight_ref, send_ref, keep_ref):
    rows, columns = send_ref.shape[0], own_ref.shape[0]
    order, up = ladder.bit(near), ladder.bit(core)
    here, there = aligned(order, columns), aligned(1 - order, columns)
    for ref, half in ((send_ref, 1 - up), (keep_ref, up)):
        part = aligned(half, rows)
        ref[...] = jnp.dot(weight_ref[part, here], own_ref[...], preferred_element_type=f32) + jnp.dot(
            weight_ref[part, there], got_ref[...], preferred_element_type=f32
        )


def project_out(ladder, near, core, own, got, weight):
    shape = jax.ShapeDtypeStruct((weight.shape[0] // 2, own.shape[1]), f32)
    return pl.pallas_call(
        functools.partial(out_kernel, ladder, near, core),
        out_shape=(shape, shape),
        in_specs=[VMEM] * 3,
        compiler_params=SMALL,
        cost_estimate=pl.CostEstimate(
            flops=2 * weight.size * own.shape[1], bytes_accessed=2 * weight.size, transcendentals=0
        ),
    )(own, got, weight)


def pack_kernel(ladder, core, keep_ref, got_ref, gain_ref, packed_ref):
    head = keep_ref[...] + got_ref[...]
    rows, width = head.shape
    gain = column(gain_ref, width)
    gain = jnp.where(ladder.bit(core) == 1, gain[rows:], gain[:rows])
    packed_ref[pl.ds(0, rows), :] = (head * gain).astype(bf16)
    square_rows(jnp.sum(head * head, axis=0, keepdims=True), packed_ref, rows)


def pack(ladder, core, keep, got, gain):
    return pl.pallas_call(
        functools.partial(pack_kernel, ladder, core),
        out_shape=jax.ShapeDtypeStruct((keep.shape[0] + EXTRA, keep.shape[1]), bf16),
        in_specs=[VMEM] * 3,
        compiler_params=SMALL,
        cost_estimate=pl.CostEstimate(flops=4 * keep.size, bytes_accessed=10 * keep.size, transcendentals=0),
    )(keep, got, gain)


def targets(ladder, core, step, places, block, count, k):
    if not places:
        return [pl.ds((k * count + p) * block, block) for p in range(count)]
    side, near = ladder.piece(core, step, k)
    result = []
    for p in range(count):
        a, b, c, d = (places[q * count + p] for q in range(4))
        place = jnp.where(side == 0, jnp.where(near == 0, a, b), jnp.where(near == 0, c, d))
        result.append(aligned(place, block))
    return result


def assemble_kernel(ladder, core, step, places, block, *refs):
    count = refs[0].shape[0] // block
    width = refs[4].shape[1]
    for k in range(4):
        for p, target in enumerate(targets(ladder, core, step, places, block, count, k)):
            value = refs[k][pl.ds(p * block, block), :]
            for c, out_ref in enumerate(refs[4:]):
                out_ref[target, :] = value[:, c * width : (c + 1) * width]


def assemble(ladder, core, step, places, block, pieces):
    rows, width = pieces[0].shape
    return pl.pallas_call(
        functools.partial(assemble_kernel, ladder, core, step, places, block),
        out_shape=[jax.ShapeDtypeStruct((4 * rows, width // CHUNKS), bf16)] * CHUNKS,
        in_specs=[VMEM] * 4,
        compiler_params=pltpu.CompilerParams(vmem_limit_bytes=8 << 20),
        cost_estimate=pl.CostEstimate(flops=0, bytes_accessed=16 * rows * width, transcendentals=0),
    )(*pieces)


def encode_kernel(ladder, core, steps, places, block, model_width, *refs):
    pieces = refs[:4]
    residual_ref, enc_ref, bias_ref, offset_ref = refs[4:8]
    hidden_ref, low_ref, slope_ref, activity_ref, base_ref, hidden_buf, sems = refs[8:]
    width = pieces[0].shape[1]
    stride = block + EXTRA
    count = pieces[0].shape[0] // stride
    tail = jnp.zeros((EXTRA, width), f32)
    for ref in pieces:
        for p in range(count):
            tail = tail + ref[pl.ds(p * stride + block, EXTRA), :].astype(f32)
    inverse = lax.rsqrt(jnp.sum(tail, axis=0, keepdims=True) / model_width + epsilon)
    for k, ref in enumerate(pieces):
        for p, target in enumerate(targets(ladder, core, steps[1], places, block, count, k)):
            value = residual_ref[target, :].astype(f32) + ref[pl.ds(p * stride, block), :].astype(f32) * inverse
            hidden_buf[target, :] = value.astype(bf16)
    store = pltpu.make_async_copy(hidden_buf, hidden_ref, sems.at[0])
    store.start()
    if places:
        mine = hidden_buf[aligned(ladder.position(steps), block), :].astype(f32)
        base_ref[...] = column(offset_ref, width) - mine
    else:
        base_ref[...] = column(offset_ref, width)
    preact = lax.dot_general(enc_ref[...], hidden_buf[...], (((0,), (0,)), ((), ())), preferred_element_type=f32)
    scaled = (preact + column(bias_ref, width)) / smoothing
    active = smoothing * (jnp.maximum(scaled, 0.0) + jnp.log1p(jnp.exp(-jnp.abs(scaled))))
    low_ref[...] = active.astype(bf16)
    slope_ref[...] = jax.nn.sigmoid(scaled)
    activity_ref[...] = jnp.sum(active, axis=1, keepdims=True)
    store.wait()


def encode(ladder, core, steps, places, block, pieces, residual, encoder, bias, offset):
    width = pieces[0].shape[1]
    model_width, latents = encoder.shape
    hbm = pl.BlockSpec(memory_space=pltpu.HBM)
    return pl.pallas_call(
        functools.partial(encode_kernel, ladder, core, steps, places, block, model_width),
        out_shape=(
            jax.ShapeDtypeStruct((model_width, width), bf16),
            jax.ShapeDtypeStruct((latents, width), bf16),
            jax.ShapeDtypeStruct((latents, width), f32),
            jax.ShapeDtypeStruct((latents, 1), f32),
            jax.ShapeDtypeStruct((offset.shape[0], width), f32),
        ),
        in_specs=[VMEM] * 8,
        out_specs=[hbm] + [VMEM] * 4,
        scratch_shapes=[pltpu.VMEM((model_width, width), bf16), pltpu.SemaphoreType.DMA((1,))],
        compiler_params=pltpu.CompilerParams(vmem_limit_bytes=2 * encoder.size + 8 * model_width * width + (4 << 20)),
        cost_estimate=pl.CostEstimate(
            flops=2 * encoder.size * width, bytes_accessed=2 * encoder.size, transcendentals=4 * latents * width
        ),
    )(*pieces, residual, encoder, bias, offset)


def decode_kernel(ladder, core, step, low_ref, peer_low_ref, dec_ref, peer_dec_any, send_ref, keep_ref, buf, sems):
    up = ladder.bit(step)
    half = send_ref.shape[0]
    first = 2 * ladder.bit(core)
    loads = []
    for i, side in enumerate((1 - up, up)):
        loads.append(pltpu.make_async_copy(peer_dec_any.at[:, aligned(first + side, half)], buf.at[i], sems.at[i]))
        loads[-1].start()
    low, peer_low = low_ref[...], peer_low_ref[...]
    tile = half // 3
    for i, (ref, side) in enumerate(((send_ref, 1 - up), (keep_ref, up))):
        loads[i].wait()
        for t in range(3):
            rows = pl.ds(t * tile, tile)
            columns = pl.ds(pl.multiple_of((first + side) * half + t * tile, tile), tile)
            value = lax.dot_general(dec_ref[:, columns], low, (((0,), (0,)), ((), ())), preferred_element_type=f32)
            value = value + lax.dot_general(
                buf[i, :, rows], peer_low, (((0,), (0,)), ((), ())), preferred_element_type=f32
            )
            ref[rows, :] = value.astype(ref.dtype)


def decode(ladder, core, step, low, peer_low, decoder, peer_decoder):
    latents, width = low.shape
    half = decoder.shape[1] // 4
    hbm = pl.BlockSpec(memory_space=pltpu.HBM)
    return pl.pallas_call(
        functools.partial(decode_kernel, ladder, core, step),
        out_shape=(jax.ShapeDtypeStruct((half, width), bf16), jax.ShapeDtypeStruct((half, width), f32)),
        in_specs=[VMEM] * 3 + [hbm],
        scratch_shapes=[pltpu.VMEM((2, latents, half), bf16), pltpu.SemaphoreType.DMA((2,))],
        compiler_params=pltpu.CompilerParams(vmem_limit_bytes=2 * decoder.size + 6 * half * width + (6 << 20)),
        cost_estimate=pl.CostEstimate(
            flops=4 * decoder.size * width, bytes_accessed=4 * decoder.size, transcendentals=0
        ),
    )(low, peer_low, decoder, in_hbm(peer_decoder))


def final_kernel(ladder, core, steps, *refs):
    chunks = CHUNKS
    errors = [refs[4 * c : 4 * c + 4] for c in range(chunks)]
    refs = refs[4 * chunks :]
    hidden_any, low, slope, activity = (refs[i * chunks : (i + 1) * chunks] for i in range(4))
    dec_ref, norm_ref, enc_out, bias_ref, dec_out = refs[4 * chunks : 4 * chunks + 5]
    hidden, error, enc_buf, dec_buf, in_sem, enc_sem, dec_sem = refs[4 * chunks + 5 :]
    width = hidden_any[0].shape[1]
    loads = []
    for c in range(chunks):
        place = hidden.at[:, pl.ds(c * width, width)]
        loads.append(pltpu.make_async_copy(hidden_any[c], place, in_sem.at[c]))
        loads[-1].start()
    quarter = errors[0][0].shape[0]
    for c in range(chunks):
        for k in range(4):
            side, near = ladder.piece(core, steps[c], k)
            error[aligned(2 * side + near, quarter), pl.ds(c * width, width)] = errors[c][k][...]
    lows = jnp.concatenate([ref[...] for ref in low], axis=1)
    slopes = jnp.concatenate([ref[...] for ref in slope], axis=1)
    norms = column(norm_ref, 128)[:, :1]
    copies = []

    def send(buf, out, index, sem):
        copies.append(pltpu.make_async_copy(buf.at[index], out.at[index], sem))
        copies[-1].start()

    tile = hidden.shape[0] // 9
    ratio = loss_weight * penalty * sum(ref[...] for ref in activity) / norms
    for t in range(9):
        columns = pl.ds(t * tile, tile)
        outer = lax.dot_general(lows, error[columns, :], (((1,), (1,)), ((), ())), preferred_element_type=f32)
        dec_buf[:, columns] = (2.0 * loss_weight * outer + ratio * dec_ref[:, columns].astype(f32)).astype(bf16)
    send(dec_buf, dec_out, slice(None), dec_sem.at[0])
    feedback = jnp.dot(dec_ref[...], error[...], preferred_element_type=f32)
    turned = (loss_weight * (2.0 * feedback + penalty * norms) * slopes).T
    bias_ref[...] = jnp.sum(turned, axis=0, keepdims=True)
    turned = turned.astype(bf16)
    for load in loads:
        load.wait()
    for t in range(9):
        rows = pl.ds(t * tile, tile)
        enc_buf[rows, :] = jnp.dot(hidden[rows, :], turned, preferred_element_type=f32).astype(bf16)
        send(enc_buf, enc_out, (rows, slice(None)), enc_sem.at[t])
    for copy in copies:
        copy.wait()


def gradients(ladder, core, steps, errors, hidden, low, slope, activity, decoder, norms):
    latents, model_width = decoder.shape
    tokens = CHUNKS * hidden[0].shape[1]
    hbm = pl.BlockSpec(memory_space=pltpu.HBM)
    flat = [piece for pieces in errors for piece in pieces]
    return pl.pallas_call(
        functools.partial(final_kernel, ladder, core, steps),
        out_shape=(
            jax.ShapeDtypeStruct((model_width, latents), bf16),
            jax.ShapeDtypeStruct((1, latents), f32),
            jax.ShapeDtypeStruct((latents, model_width), bf16),
        ),
        in_specs=[VMEM] * len(flat) + [hbm] * CHUNKS + [VMEM] * (3 * CHUNKS + 2),
        out_specs=(hbm, VMEM, hbm),
        scratch_shapes=[
            pltpu.VMEM((model_width, tokens), bf16),
            pltpu.VMEM((model_width, tokens), bf16),
            pltpu.VMEM((model_width, latents), bf16),
            pltpu.VMEM((latents, model_width), bf16),
            pltpu.SemaphoreType.DMA((CHUNKS,)),
            pltpu.SemaphoreType.DMA((9,)),
            pltpu.SemaphoreType.DMA((1,)),
        ],
        compiler_params=pltpu.CompilerParams(
            vmem_limit_bytes=4 * decoder.size + 4 * model_width * tokens + (6 << 20)
        ),
        cost_estimate=pl.CostEstimate(
            flops=6 * decoder.size * tokens, bytes_accessed=12 * decoder.size, transcendentals=0
        ),
    )(*flat, *hidden, *low, *slope, *activity, decoder, norms)


def split_rows(value):
    high = lax.reduce_precision(value, 8, 7)
    rows = jnp.concatenate([high, value - high], axis=0).astype(bf16)
    return jnp.concatenate([rows, jnp.zeros((EXTRA - 2, value.shape[1]), bf16)], axis=0)


def on_device(ladder, residual, norm_gain, query_weight, key_weight, value_weight, out_weight, post_gain,
              encoder_weight, encoder_bias, decoder_weight, decoder_bias):
    tokens = residual.shape[0]
    model_width = decoder_weight.shape[1]
    groups = key_weight.shape[1] // HEAD_DIM
    heads = query_weight.shape[1] // key_weight.shape[1]
    width = tokens // CHUNKS
    cuts = [slice(c * width, (c + 1) * width) for c in range(CHUNKS)]

    cores = ladder.cores
    dp_steps = ladder.route((0, 1, 2), (1, 0, 2))
    routes = [ladder.route((0, 1, 2), (1, 2, 0)), ladder.route((2, 0, 1), (1, 0, 2))]
    group_bits = groups.bit_length() - 1
    assert groups == 1 << group_bits and group_bits <= len(dp_steps)
    group_steps, copy_steps = dp_steps[:group_bits], dp_steps[group_bits:]

    residual_t = residual.T
    core = cores[0]
    core_bit = ladder.bit(core)
    paired = len(cores) == 1 and residual_t.shape[0] % 32 == 0 and group_bits >= 1

    mine, gain = residual_t, post_gain[:, None]
    for step in cores:
        half = mine.shape[0] // 2
        up = ladder.bit(step) == 1
        mine = jnp.where(up, mine[half:], mine[:half])
        gain = jnp.where(up, gain[half:], gain[:half])
    block = mine.shape[0]

    def canonical(pieces, steps, stride):
        own, far, own_peer, far_peer = pieces
        value = []
        for k, (a, b) in ((0, (own, far)), (2, (own_peer, far_peer))):
            _, near = ladder.piece(core, steps[0], k)
            value.append(jnp.concatenate([jnp.where(near == 1, b, a), jnp.where(near == 1, a, b)], axis=0))
        own, got = value
        value = jnp.concatenate([jnp.where(core_bit == 1, got, own), jnp.where(core_bit == 1, own, got)], axis=0)
        order = ladder.order(cores[:1] + steps)
        return jnp.concatenate(
            [value[p * stride : p * stride + block] for p in (order.index(i) for i in range(len(order)))], axis=0
        )

    def cut_four(value):
        quarter = value.shape[0] // 4
        return [value[k * quarter : (k + 1) * quarter] for k in range(4)]

    half_dim = HEAD_DIM // 2
    frequency = rope_base ** (-2.0 * jnp.arange(half_dim, dtype=f32) / HEAD_DIM)
    angles = frequency[:, None] * jnp.arange(tokens).astype(f32)[None, :]
    cosine, sine = jnp.cos(angles), jnp.sin(angles)

    out_t = out_weight.T
    decoder_peer = ladder.swap(decoder_weight, core)
    encoder_near, decoder_near = in_vmem(encoder_weight), in_vmem(decoder_weight)
    norms = jnp.sqrt(jnp.sum(jnp.square(decoder_weight.astype(f32)), axis=1) + epsilon)

    if paired:
        sends, keeps, squares = project(
            ladder, dp_steps[0], groups, heads, residual_t, norm_gain, query_weight, key_weight, value_weight
        )
    else:
        residual_float = residual_t.astype(f32)
        scaled = (residual_float * norm_gain[:, None]).astype(bf16)
        square = jnp.sum(residual_float * residual_float, axis=0, keepdims=True)
        pieces = []
        for g in range(groups):
            pieces += [
                query_weight[:, g * heads * HEAD_DIM : (g + 1) * heads * HEAD_DIM],
                key_weight[:, g * HEAD_DIM : (g + 1) * HEAD_DIM],
                value_weight[:, g * HEAD_DIM : (g + 1) * HEAD_DIM],
            ]
        stacked = jnp.concatenate(pieces, axis=1)
        projected = lax.dot_general(stacked, scaled, (((0,), (0,)), ((), ())), preferred_element_type=f32)
        sends, keeps, squares = [], [], []
        for cut in cuts:
            send = keep = projected[:, cut]
            if group_bits:
                half = send.shape[0] // 2
                up = ladder.bit(dp_steps[0]) == 1
                send, keep = jnp.where(up, keep[:half], keep[half:]), jnp.where(up, keep[half:], keep[:half])
            sends.append(jnp.concatenate([send.astype(bf16), split_rows(square[:, cut])], axis=0))
            keeps.append(keep)
            squares.append(square[:, cut])

    sends[0], mine = lax.optimization_barrier((sends[0], mine))
    steps = cores[1:] + routes[0]
    residual_own = ladder.gather(mine, steps[1:])
    residual_far = ladder.swap(residual_own, steps[0])
    old = ()
    attendeds = []
    errors, nears, hiddens, lows, slopes, activities = [], [], [], [], [], []
    for c in range(CHUNKS):
        send, part, square = sends[c], keeps[c], squares[c]
        for i, step in enumerate(dp_steps):
            got = ladder.swap(send, step)
            if i < len(dp_steps) - 1:
                send, part, square = advance(ladder, dp_steps[i + 1], i + 1 < group_bits, part, got, square)
        attended, *old = attend(c * width, heads, model_width, part, got, square, cosine, sine, *old)
        attendeds.append(attended)

    residuals = (residual_own, residual_far, ladder.swap(residual_own, core), ladder.swap(residual_far, core))
    if paired:
        residual_all = assemble(ladder, core, steps[0], ladder.order(cores + routes[0]), block, residuals)
    else:
        residual_all = canonical(residuals, steps, block)
        residual_all = [residual_all[:, cut] for cut in cuts]

    slots = [ladder.position(cores + routes[c % len(routes)]) * block for c in range(CHUNKS)]
    offsets = [lax.dynamic_slice_in_dim(decoder_bias, slot, block) for slot in slots]
    for c, attended in enumerate(attendeds):
        if paired:
            attended = ladder.gather(attended, group_steps[1:])
            got = ladder.swap(attended, group_steps[0])
            send, keep = project_out(ladder, group_steps[0], core, attended, got, out_t)
            packed = pack(ladder, core, keep, ladder.swap(send, core), post_gain)
        else:
            attended = ladder.gather(attended, group_steps)
            head = ladder.scatter(jnp.dot(out_t, attended, preferred_element_type=f32), cores, f32)
            packed = jnp.concatenate(
                [(head * gain).astype(bf16), split_rows(jnp.sum(head * head, axis=0, keepdims=True))], axis=0
            )
        steps = routes[c % len(routes)]
        path = cores[1:] + steps
        own = ladder.gather(packed, path[1:])
        if c == 1:
            own, norms, offsets, residual_all = lax.optimization_barrier((own, norms, offsets, residual_all))
        far = ladder.swap(own, path[0])
        pieces = own, far, ladder.swap(own, core), ladder.swap(far, core)
        near = (cores[1:] + steps)[0]
        kernel_block, places = block, ladder.order(cores + steps)
        if not paired:
            stride = block + EXTRA
            tails = sum(
                v[p * stride + block : (p + 1) * stride].astype(f32)
                for v in pieces
                for p in range(v.shape[0] // stride)
            )
            tails = split_rows(jnp.sum(tails, axis=0, keepdims=True))
            whole = cut_four(canonical(pieces, cores[1:] + steps, stride))
            pieces = [
                jnp.concatenate([v, tails if k == 0 else jnp.zeros_like(tails)], axis=0) for k, v in enumerate(whole)
            ]
            kernel_block, places = model_width // 4, ()
        slot, offset = slots[c], offsets[c]
        hidden, low, slope, activity, base = encode(
            ladder, core, cores + steps, places, kernel_block, pieces, residual_all[c], encoder_near, encoder_bias, offset
        )
        if not paired:
            base = base - lax.dynamic_slice_in_dim(hidden, slot, block, axis=0).astype(f32)
        send, part = decode(ladder, core, path[0], low, ladder.swap(low, core), decoder_near, decoder_peer)
        part = part + ladder.swap(send, path[0]).astype(f32)
        error = (ladder.scatter(part, path[1:], bf16) + base).astype(bf16)
        errors.append(ladder.quarters(error, core, cores[1:] + steps))
        nears.append(near)
        hiddens.append(hidden)
        lows.append(low)
        slopes.append(slope)
        activities.append(activity)

    encoder_grad, encoder_bias_grad, decoder_grad = gradients(
        ladder, core, nears, errors, hiddens, lows, slopes, activities, decoder_near, norms
    )
    return encoder_grad, encoder_bias_grad[0], decoder_grad


def solution(mesh):
    ladder = Ladder(mesh.shape["dp"], mesh.shape["mp"])
    placed = (
        P(None, "dp"),
        P("dp"),
        P("dp", "mp"),
        P("dp", "mp"),
        P("dp", "mp"),
        P("mp", "dp"),
        P("dp"),
        P(None, ("dp", "mp")),
        P(("dp", "mp")),
        P(("dp", "mp"), None),
        P(),
    )
    return jax.shard_map(
        functools.partial(on_device, ladder),
        mesh=mesh,
        in_specs=placed,
        out_specs=(P(None, ("dp", "mp")), P(("dp", "mp")), P(("dp", "mp"), None)),
        check_vma=False,
    )
```

```python
import functools

import jax
import jax.numpy as jnp
from jax import lax
from jax.experimental import pallas as pl
from jax.experimental.pallas import tpu as pltpu
from jax.sharding import PartitionSpec as P

HEAD_DIM = 128
CHUNKS = 2
EXTRA = 16

epsilon = 1e-06
softcap = 50.0
query_scale = 1.0 / 12.0
rope_base = 10000.0
smoothing = 0.1
penalty = 1.0
loss_weight = 0.0625

bf16 = jnp.bfloat16
f32 = jnp.float32
AXES = ("dp", "mp")


class Ladder:
    def __init__(self, dp, mp):
        self.dp, self.mp = dp, mp
        dp_bits, mp_bits = dp.bit_length() - 1, mp.bit_length() - 1
        assert dp == 1 << dp_bits and mp == 1 << mp_bits
        self.dp_bits = dp_bits
        self.cores = [(("mp", k), ("mp", k)) for k in range(mp_bits - 1, -1, -1)]

    def route(self, even, odd):
        if self.dp_bits < len(even):
            even = odd = tuple(range(self.dp_bits))
        rest = tuple(range(len(even), self.dp_bits))
        return [(("dp", j), ("dp", k)) for j, k in zip(even + rest, odd + rest)]

    def pairs(self, step):
        result = []
        for d in range(self.dp):
            for m in range(self.mp):
                axis, k = step[m & 1]
                peer = (d ^ (1 << k), m) if axis == "dp" else (d, m ^ (1 << k))
                result.append((d * self.mp + m, peer[0] * self.mp + peer[1]))
        return result

    def static_bit(self, step, d, m):
        axis, k = step[m & 1]
        return ((d if axis == "dp" else m) >> k) & 1

    def bit(self, step):
        d, m = lax.axis_index("dp"), lax.axis_index("mp")
        (axis, even), (_, odd) = step
        value = d if axis == "dp" else m
        if even == odd:
            return (value >> even) & 1
        return jnp.where(m & 1 == 0, (value >> even) & 1, (value >> odd) & 1)

    def swap(self, value, step):
        return lax.ppermute(value, AXES, self.pairs(step))

    def scatter(self, value, steps, wire):
        for step in steps:
            half = value.shape[0] // 2
            up = self.bit(step) == 1
            low, high = value[:half], value[half:]
            got = self.swap(jnp.where(up, low, high).astype(wire), step)
            value = jnp.where(up, high, low) + got.astype(f32)
        return value

    def gather(self, value, steps):
        for step in reversed(steps):
            got = self.swap(value, step)
            up = self.bit(step) == 1
            value = jnp.concatenate([jnp.where(up, got, value), jnp.where(up, value, got)], axis=0)
        return value

    def quarters(self, value, core, steps):
        own = self.gather(value, steps[1:])
        far = self.swap(own, steps[0])
        return own, far, self.swap(own, core), self.swap(far, core)

    def order(self, steps):
        where = {}
        for d in range(self.dp):
            for m in range(self.mp):
                p = 0
                for step in steps:
                    p = 2 * p + self.static_bit(step, d, m)
                where[p] = d * self.mp + m
        return [where[p] for p in range(self.dp * self.mp)]

    def position(self, steps):
        p = 0
        for step in steps:
            p = 2 * p + self.bit(step)
        return p

    def piece(self, core, step, k):
        up = self.bit(core)
        if k < 2:
            near = self.bit(step)
            return up, near if k == 0 else 1 - near
        d, m = lax.axis_index("dp"), lax.axis_index("mp") ^ (1 << core[0][1])
        (axis, even), (_, odd) = step
        value = d if axis == "dp" else m
        near = jnp.where(m & 1 == 0, (value >> even) & 1, (value >> odd) & 1)
        return 1 - up, near if k == 2 else 1 - near


VMEM = pl.BlockSpec(memory_space=pltpu.VMEM)


def in_hbm(value):
    return pltpu.with_memory_space_constraint(value, pltpu.HBM)


def in_vmem(value):
    return pltpu.with_memory_space_constraint(value, pltpu.VMEM)


SMALL = pltpu.CompilerParams(vmem_limit_bytes=6 << 20)


def aligned(index, size):
    return pl.ds(pl.multiple_of(index * size, size), size)


def square_rows(total, ref, first):
    high = total.astype(bf16).astype(f32)
    place = lax.broadcasted_iota(jnp.int32, (EXTRA, total.shape[1]), 0)
    rows = jnp.where(place == 0, high, jnp.where(place == 1, total - high, 0.0))
    ref[pl.ds(first, EXTRA), :] = rows.astype(bf16)


def column(ref, width):
    return jnp.broadcast_to(ref[...][None, :], (width, ref.shape[0])).T


def project_kernel(ladder, step, groups, heads, chunks, residual_ref, gain_ref, *refs):
    weights, outs = refs[:3], refs[3 : 3 + 3 * chunks]
    query_ref, key_ref, value_ref = refs[-4:-1]
    copies = [pltpu.make_async_copy(w, r, refs[-1].at[i]) for i, (w, r) in enumerate(zip(weights, refs[-4:-1]))]
    for copy in copies:
        copy.start()
    up = ladder.bit(step)
    tokens = residual_ref.shape[1]
    width = tokens // chunks
    wide = heads * HEAD_DIM
    residual = residual_ref[...].astype(f32)
    scaled = (residual * column(gain_ref, tokens)).astype(bf16)
    square = jnp.sum(residual * residual, axis=0, keepdims=True)
    for copy in copies:
        copy.wait()
    sends, keeps, squares = outs[:chunks], outs[chunks : 2 * chunks], outs[2 * chunks :]
    half = groups // 2

    def times(weight):
        return lax.dot_general(weight, scaled, (((0,), (0,)), ((), ())), preferred_element_type=f32)

    for refs, side in ((sends, 1 - up), (keeps, up)):
        for j in range(half):
            g = side * half + j
            first = j * (wide + 2 * HEAD_DIM)
            for weight, size in ((query_ref, wide), (key_ref, HEAD_DIM), (value_ref, HEAD_DIM)):
                value = times(weight[:, aligned(g, size)])
                for c, ref in enumerate(refs):
                    ref[pl.ds(first, size), :] = value[:, c * width : (c + 1) * width].astype(ref.dtype)
                first += size
    for c in range(chunks):
        part = square[:, c * width : (c + 1) * width]
        squares[c][...] = part
        square_rows(part, sends[c], half * (wide + 2 * HEAD_DIM))


def project(ladder, step, groups, heads, residual, gain, query, key, value):
    width = residual.shape[1] // CHUNKS
    rows = groups // 2 * (heads + 2) * HEAD_DIM
    shapes = (
        [jax.ShapeDtypeStruct((rows + EXTRA, width), bf16)] * CHUNKS
        + [jax.ShapeDtypeStruct((rows, width), f32)] * CHUNKS
        + [jax.ShapeDtypeStruct((1, width), f32)] * CHUNKS
    )
    outs = pl.pallas_call(
        functools.partial(project_kernel, ladder, step, groups, heads, CHUNKS),
        out_shape=shapes,
        in_specs=[VMEM] * 2 + [pl.BlockSpec(memory_space=pltpu.HBM)] * 3,
        scratch_shapes=[
            pltpu.VMEM(query.shape, bf16),
            pltpu.VMEM(key.shape, bf16),
            pltpu.VMEM(value.shape, bf16),
            pltpu.SemaphoreType.DMA((3,)),
        ],
        compiler_params=pltpu.CompilerParams(vmem_limit_bytes=10 << 20),
        cost_estimate=pl.CostEstimate(
            flops=4 * rows * residual.size, bytes_accessed=2 * (query.size + key.size + value.size), transcendentals=0
        ),
    )(residual, gain, in_hbm(query), in_hbm(key), in_hbm(value))
    return list(outs[:CHUNKS]), outs[CHUNKS : 2 * CHUNKS], outs[2 * CHUNKS :]


def step_kernel(ladder, step, halve, own_ref, got_ref, square_ref, send_ref, keep_ref, total_ref):
    rows, kept = own_ref.shape[0], keep_ref.shape[0]
    total = square_ref[...] + jnp.sum(got_ref[pl.ds(rows, EXTRA), :].astype(f32), axis=0, keepdims=True)
    total_ref[...] = total
    square_rows(total, send_ref, kept)
    if halve:
        up = ladder.bit(step)
        here, there = aligned(up, kept), aligned(1 - up, kept)
        send_ref[pl.ds(0, kept), :] = (own_ref[there, :] + got_ref[there, :].astype(f32)).astype(bf16)
        keep_ref[...] = own_ref[here, :] + got_ref[here, :].astype(f32)
    else:
        value = own_ref[...] + got_ref[pl.ds(0, rows), :].astype(f32)
        send_ref[pl.ds(0, kept), :] = value.astype(bf16)
        keep_ref[...] = value


def advance(ladder, step, halve, own, got, square):
    rows, width = own.shape
    kept = rows // 2 if halve else rows
    return pl.pallas_call(
        functools.partial(step_kernel, ladder, step, halve),
        out_shape=(
            jax.ShapeDtypeStruct((kept + EXTRA, width), bf16),
            jax.ShapeDtypeStruct((kept, width), f32),
            jax.ShapeDtypeStruct((1, width), f32),
        ),
        in_specs=[VMEM] * 3,
        compiler_params=SMALL,
        cost_estimate=pl.CostEstimate(flops=2 * own.size, bytes_accessed=12 * own.size, transcendentals=0),
    )(own, got, square)


def attention_kernel(start, heads, model_width, own_ref, got_ref, square_ref, cos_ref, sin_ref, *refs):
    oldk_ref, oldv_ref = refs[:2] if start else (None, None)
    out_ref, k_ref, v_ref = refs[-3:]
    width = own_ref.shape[1]
    half = HEAD_DIM // 2
    body = own_ref.shape[0]
    tail = jnp.sum(got_ref[pl.ds(body, EXTRA), :].astype(f32), axis=0, keepdims=True)
    inverse = lax.rsqrt((square_ref[...] + tail) / model_width + epsilon)
    lanes = pl.ds(start, width)
    cosine, sine = cos_ref[:, lanes], sin_ref[:, lanes]

    def rows(first, count):
        return (own_ref[pl.ds(first, count), :] + got_ref[pl.ds(first, count), :].astype(f32)) * inverse

    def rotated(first):
        front, back = rows(first, half), rows(first + half, half)
        return jnp.concatenate([front * cosine - back * sine, back * cosine + front * sine], axis=0).astype(bf16)

    base = heads * HEAD_DIM
    k_ref[:, pl.ds(start, width)] = rotated(base)
    v_ref[:, pl.ds(start, width)] = rows(base + HEAD_DIM, HEAD_DIM).astype(bf16)
    if start:
        k_ref[:, pl.ds(0, start)] = oldk_ref[...]
        v_ref[:, pl.ds(0, start)] = oldv_ref[...]
    keys, values = k_ref[...], v_ref[...]
    span = start + width
    allowed = lax.broadcasted_iota(jnp.int32, (span, width), 0) <= lax.broadcasted_iota(jnp.int32, (span, width), 1) + start
    for h in range(heads):
        query = rotated(h * HEAD_DIM)
        score = lax.dot_general(keys, query, (((0,), (0,)), ((), ())), preferred_element_type=f32) * query_scale
        capped = softcap * jnp.tanh(score / softcap)
        weights = jnp.where(allowed, jnp.exp(capped), 0.0)
        total = jnp.sum(weights, axis=0, keepdims=True)
        mixed = jnp.dot(values, weights.astype(bf16), preferred_element_type=f32)
        out_ref[pl.ds(h * HEAD_DIM, HEAD_DIM), :] = (mixed / total).astype(bf16)


def attend(start, heads, model_width, own, got, square, cosine, sine, *old):
    width = own.shape[1]
    span = start + width
    return pl.pallas_call(
        functools.partial(attention_kernel, start, heads, model_width),
        out_shape=(
            jax.ShapeDtypeStruct((heads * HEAD_DIM, width), bf16),
            jax.ShapeDtypeStruct((HEAD_DIM, span), bf16),
            jax.ShapeDtypeStruct((HEAD_DIM, span), bf16),
        ),
        compiler_params=SMALL,
        cost_estimate=pl.CostEstimate(
            flops=4 * heads * HEAD_DIM * span * width, bytes_accessed=8 * own.size, transcendentals=2 * heads * span * width
        ),
    )(own, got, square, cosine, sine, *old)


def out_kernel(ladder, near, core, own_ref, got_ref, weight_ref, send_ref, keep_ref):
    rows, columns = send_ref.shape[0], own_ref.shape[0]
    order, up = ladder.bit(near), ladder.bit(core)
    here, there = aligned(order, columns), aligned(1 - order, columns)
    for ref, half in ((send_ref, 1 - up), (keep_ref, up)):
        part = aligned(half, rows)
        ref[...] = jnp.dot(weight_ref[part, here], own_ref[...], preferred_element_type=f32) + jnp.dot(
            weight_ref[part, there], got_ref[...], preferred_element_type=f32
        )


def project_out(ladder, near, core, own, got, weight):
    shape = jax.ShapeDtypeStruct((weight.shape[0] // 2, own.shape[1]), f32)
    return pl.pallas_call(
        functools.partial(out_kernel, ladder, near, core),
        out_shape=(shape, shape),
        in_specs=[VMEM] * 3,
        compiler_params=SMALL,
        cost_estimate=pl.CostEstimate(
            flops=2 * weight.size * own.shape[1], bytes_accessed=2 * weight.size, transcendentals=0
        ),
    )(own, got, weight)


def pack_kernel(ladder, core, keep_ref, got_ref, gain_ref, packed_ref):
    head = keep_ref[...] + got_ref[...]
    rows, width = head.shape
    gain = column(gain_ref, width)
    gain = jnp.where(ladder.bit(core) == 1, gain[rows:], gain[:rows])
    packed_ref[pl.ds(0, rows), :] = (head * gain).astype(bf16)
    square_rows(jnp.sum(head * head, axis=0, keepdims=True), packed_ref, rows)


def pack(ladder, core, keep, got, gain):
    return pl.pallas_call(
        functools.partial(pack_kernel, ladder, core),
        out_shape=jax.ShapeDtypeStruct((keep.shape[0] + EXTRA, keep.shape[1]), bf16),
        in_specs=[VMEM] * 3,
        compiler_params=SMALL,
        cost_estimate=pl.CostEstimate(flops=4 * keep.size, bytes_accessed=10 * keep.size, transcendentals=0),
    )(keep, got, gain)


def targets(ladder, core, step, places, block, count, k):
    if not places:
        return [pl.ds((k * count + p) * block, block) for p in range(count)]
    side, near = ladder.piece(core, step, k)
    result = []
    for p in range(count):
        a, b, c, d = (places[q * count + p] for q in range(4))
        place = jnp.where(side == 0, jnp.where(near == 0, a, b), jnp.where(near == 0, c, d))
        result.append(aligned(place, block))
    return result


def assemble_kernel(ladder, core, step, places, block, *refs):
    count = refs[0].shape[0] // block
    width = refs[4].shape[1]
    for k in range(4):
        for p, target in enumerate(targets(ladder, core, step, places, block, count, k)):
            value = refs[k][pl.ds(p * block, block), :]
            for c, out_ref in enumerate(refs[4:]):
                out_ref[target, :] = value[:, c * width : (c + 1) * width]


def assemble(ladder, core, step, places, block, pieces):
    rows, width = pieces[0].shape
    return pl.pallas_call(
        functools.partial(assemble_kernel, ladder, core, step, places, block),
        out_shape=[jax.ShapeDtypeStruct((4 * rows, width // CHUNKS), bf16)] * CHUNKS,
        in_specs=[VMEM] * 4,
        compiler_params=pltpu.CompilerParams(vmem_limit_bytes=8 << 20),
        cost_estimate=pl.CostEstimate(flops=0, bytes_accessed=16 * rows * width, transcendentals=0),
    )(*pieces)


def encode_kernel(ladder, core, steps, places, block, model_width, *refs):
    pieces = refs[:4]
    residual_ref, enc_ref, bias_ref, offset_ref = refs[4:8]
    hidden_ref, low_ref, slope_ref, activity_ref, base_ref, hidden_buf, sems = refs[8:]
    width = pieces[0].shape[1]
    stride = block + EXTRA
    count = pieces[0].shape[0] // stride
    tail = jnp.zeros((EXTRA, width), f32)
    for ref in pieces:
        for p in range(count):
            tail = tail + ref[pl.ds(p * stride + block, EXTRA), :].astype(f32)
    inverse = lax.rsqrt(jnp.sum(tail, axis=0, keepdims=True) / model_width + epsilon)
    for k, ref in enumerate(pieces):
        for p, target in enumerate(targets(ladder, core, steps[1], places, block, count, k)):
            value = residual_ref[target, :].astype(f32) + ref[pl.ds(p * stride, block), :].astype(f32) * inverse
            hidden_buf[target, :] = value.astype(bf16)
    store = pltpu.make_async_copy(hidden_buf, hidden_ref, sems.at[0])
    store.start()
    if places:
        mine = hidden_buf[aligned(ladder.position(steps), block), :].astype(f32)
        base_ref[...] = column(offset_ref, width) - mine
    else:
        base_ref[...] = column(offset_ref, width)
    preact = lax.dot_general(enc_ref[...], hidden_buf[...], (((0,), (0,)), ((), ())), preferred_element_type=f32)
    scaled = (preact + column(bias_ref, width)) / smoothing
    active = smoothing * (jnp.maximum(scaled, 0.0) + jnp.log1p(jnp.exp(-jnp.abs(scaled))))
    low_ref[...] = active.astype(bf16)
    slope_ref[...] = jax.nn.sigmoid(scaled)
    activity_ref[...] = jnp.sum(active, axis=1, keepdims=True)
    store.wait()


def encode(ladder, core, steps, places, block, pieces, residual, encoder, bias, offset):
    width = pieces[0].shape[1]
    model_width, latents = encoder.shape
    hbm = pl.BlockSpec(memory_space=pltpu.HBM)
    return pl.pallas_call(
        functools.partial(encode_kernel, ladder, core, steps, places, block, model_width),
        out_shape=(
            jax.ShapeDtypeStruct((model_width, width), bf16),
            jax.ShapeDtypeStruct((latents, width), bf16),
            jax.ShapeDtypeStruct((latents, width), f32),
            jax.ShapeDtypeStruct((latents, 1), f32),
            jax.ShapeDtypeStruct((offset.shape[0], width), f32),
        ),
        in_specs=[VMEM] * 8,
        out_specs=[hbm] + [VMEM] * 4,
        scratch_shapes=[pltpu.VMEM((model_width, width), bf16), pltpu.SemaphoreType.DMA((1,))],
        compiler_params=pltpu.CompilerParams(vmem_limit_bytes=2 * encoder.size + 8 * model_width * width + (4 << 20)),
        cost_estimate=pl.CostEstimate(
            flops=2 * encoder.size * width, bytes_accessed=2 * encoder.size, transcendentals=4 * latents * width
        ),
    )(*pieces, residual, encoder, bias, offset)


def decode_kernel(ladder, core, step, low_ref, peer_low_ref, dec_ref, peer_dec_any, send_ref, keep_ref, buf, sems):
    up = ladder.bit(step)
    half = send_ref.shape[0]
    first = 2 * ladder.bit(core)
    loads = []
    for i, side in enumerate((1 - up, up)):
        loads.append(pltpu.make_async_copy(peer_dec_any.at[:, aligned(first + side, half)], buf.at[i], sems.at[i]))
        loads[-1].start()
    low, peer_low = low_ref[...], peer_low_ref[...]
    tile = half // 3
    for i, (ref, side) in enumerate(((send_ref, 1 - up), (keep_ref, up))):
        loads[i].wait()
        for t in range(3):
            rows = pl.ds(t * tile, tile)
            columns = pl.ds(pl.multiple_of((first + side) * half + t * tile, tile), tile)
            value = lax.dot_general(dec_ref[:, columns], low, (((0,), (0,)), ((), ())), preferred_element_type=f32)
            value = value + lax.dot_general(
                buf[i, :, rows], peer_low, (((0,), (0,)), ((), ())), preferred_element_type=f32
            )
            ref[rows, :] = value.astype(ref.dtype)


def decode(ladder, core, step, low, peer_low, decoder, peer_decoder):
    latents, width = low.shape
    half = decoder.shape[1] // 4
    hbm = pl.BlockSpec(memory_space=pltpu.HBM)
    return pl.pallas_call(
        functools.partial(decode_kernel, ladder, core, step),
        out_shape=(jax.ShapeDtypeStruct((half, width), bf16), jax.ShapeDtypeStruct((half, width), f32)),
        in_specs=[VMEM] * 3 + [hbm],
        scratch_shapes=[pltpu.VMEM((2, latents, half), bf16), pltpu.SemaphoreType.DMA((2,))],
        compiler_params=pltpu.CompilerParams(vmem_limit_bytes=2 * decoder.size + 6 * half * width + (6 << 20)),
        cost_estimate=pl.CostEstimate(
            flops=4 * decoder.size * width, bytes_accessed=4 * decoder.size, transcendentals=0
        ),
    )(low, peer_low, decoder, in_hbm(peer_decoder))


def final_kernel(ladder, core, steps, *refs):
    chunks = CHUNKS
    errors = [refs[4 * c : 4 * c + 4] for c in range(chunks)]
    refs = refs[4 * chunks :]
    hidden_any, low, slope, activity = (refs[i * chunks : (i + 1) * chunks] for i in range(4))
    dec_ref, norm_ref, enc_out, bias_ref, dec_out = refs[4 * chunks : 4 * chunks + 5]
    hidden, error, enc_buf, dec_buf, in_sem, enc_sem, dec_sem = refs[4 * chunks + 5 :]
    width = hidden_any[0].shape[1]
    loads = []
    for c in range(chunks):
        place = hidden.at[:, pl.ds(c * width, width)]
        loads.append(pltpu.make_async_copy(hidden_any[c], place, in_sem.at[c]))
        loads[-1].start()
    quarter = errors[0][0].shape[0]
    for c in range(chunks):
        for k in range(4):
            side, near = ladder.piece(core, steps[c], k)
            error[aligned(2 * side + near, quarter), pl.ds(c * width, width)] = errors[c][k][...]
    lows = jnp.concatenate([ref[...] for ref in low], axis=1)
    slopes = jnp.concatenate([ref[...] for ref in slope], axis=1)
    norms = column(norm_ref, 128)[:, :1]
    copies = []

    def send(buf, out, index, sem):
        copies.append(pltpu.make_async_copy(buf.at[index], out.at[index], sem))
        copies[-1].start()

    tile = hidden.shape[0] // 9
    ratio = loss_weight * penalty * sum(ref[...] for ref in activity) / norms
    for t in range(9):
        columns = pl.ds(t * tile, tile)
        outer = lax.dot_general(lows, error[columns, :], (((1,), (1,)), ((), ())), preferred_element_type=f32)
        dec_buf[:, columns] = (2.0 * loss_weight * outer + ratio * dec_ref[:, columns].astype(f32)).astype(bf16)
    send(dec_buf, dec_out, slice(None), dec_sem.at[0])
    feedback = jnp.dot(dec_ref[...], error[...], preferred_element_type=f32)
    turned = (loss_weight * (2.0 * feedback + penalty * norms) * slopes).T
    bias_ref[...] = jnp.sum(turned, axis=0, keepdims=True)
    turned = turned.astype(bf16)
    for load in loads:
        load.wait()
    for t in range(9):
        rows = pl.ds(t * tile, tile)
        enc_buf[rows, :] = jnp.dot(hidden[rows, :], turned, preferred_element_type=f32).astype(bf16)
        send(enc_buf, enc_out, (rows, slice(None)), enc_sem.at[t])
    for copy in copies:
        copy.wait()


def gradients(ladder, core, steps, errors, hidden, low, slope, activity, decoder, norms):
    latents, model_width = decoder.shape
    tokens = CHUNKS * hidden[0].shape[1]
    hbm = pl.BlockSpec(memory_space=pltpu.HBM)
    flat = [piece for pieces in errors for piece in pieces]
    return pl.pallas_call(
        functools.partial(final_kernel, ladder, core, steps),
        out_shape=(
            jax.ShapeDtypeStruct((model_width, latents), bf16),
            jax.ShapeDtypeStruct((1, latents), f32),
            jax.ShapeDtypeStruct((latents, model_width), bf16),
        ),
        in_specs=[VMEM] * len(flat) + [hbm] * CHUNKS + [VMEM] * (3 * CHUNKS + 2),
        out_specs=(hbm, VMEM, hbm),
        scratch_shapes=[
            pltpu.VMEM((model_width, tokens), bf16),
            pltpu.VMEM((model_width, tokens), bf16),
            pltpu.VMEM((model_width, latents), bf16),
            pltpu.VMEM((latents, model_width), bf16),
            pltpu.SemaphoreType.DMA((CHUNKS,)),
            pltpu.SemaphoreType.DMA((9,)),
            pltpu.SemaphoreType.DMA((1,)),
        ],
        compiler_params=pltpu.CompilerParams(
            vmem_limit_bytes=4 * decoder.size + 4 * model_width * tokens + (6 << 20)
        ),
        cost_estimate=pl.CostEstimate(
            flops=6 * decoder.size * tokens, bytes_accessed=12 * decoder.size, transcendentals=0
        ),
    )(*flat, *hidden, *low, *slope, *activity, decoder, norms)


def split_rows(value):
    high = lax.reduce_precision(value, 8, 7)
    rows = jnp.concatenate([high, value - high], axis=0).astype(bf16)
    return jnp.concatenate([rows, jnp.zeros((EXTRA - 2, value.shape[1]), bf16)], axis=0)


def on_device(ladder, residual, norm_gain, query_weight, key_weight, value_weight, out_weight, post_gain,
              encoder_weight, encoder_bias, decoder_weight, decoder_bias):
    tokens = residual.shape[0]
    model_width = decoder_weight.shape[1]
    groups = key_weight.shape[1] // HEAD_DIM
    heads = query_weight.shape[1] // key_weight.shape[1]
    width = tokens // CHUNKS
    cuts = [slice(c * width, (c + 1) * width) for c in range(CHUNKS)]

    cores = ladder.cores
    dp_steps = ladder.route((0, 1, 2), (1, 0, 2))
    routes = [ladder.route((0, 1, 2), (1, 2, 0)), ladder.route((2, 0, 1), (1, 0, 2))]
    group_bits = groups.bit_length() - 1
    assert groups == 1 << group_bits and group_bits <= len(dp_steps)
    group_steps, copy_steps = dp_steps[:group_bits], dp_steps[group_bits:]

    residual_t = residual.T
    core = cores[0]
    core_bit = ladder.bit(core)
    paired = len(cores) == 1 and residual_t.shape[0] % 32 == 0 and group_bits >= 1

    def share(value):
        for step in cores:
            half = value.shape[0] // 2
            value = jnp.where(ladder.bit(step) == 1, value[half:], value[:half])
        return value

    gain = share(post_gain[:, None])
    block = gain.shape[0]

    def canonical(pieces, steps, stride):
        own, far, own_peer, far_peer = pieces
        value = []
        for k, (a, b) in ((0, (own, far)), (2, (own_peer, far_peer))):
            _, near = ladder.piece(core, steps[0], k)
            value.append(jnp.concatenate([jnp.where(near == 1, b, a), jnp.where(near == 1, a, b)], axis=0))
        own, got = value
        value = jnp.concatenate([jnp.where(core_bit == 1, got, own), jnp.where(core_bit == 1, own, got)], axis=0)
        order = ladder.order(cores[:1] + steps)
        return jnp.concatenate(
            [value[p * stride : p * stride + block] for p in (order.index(i) for i in range(len(order)))], axis=0
        )

    def cut_four(value):
        quarter = value.shape[0] // 4
        return [value[k * quarter : (k + 1) * quarter] for k in range(4)]

    half_dim = HEAD_DIM // 2
    frequency = rope_base ** (-2.0 * jnp.arange(half_dim, dtype=f32) / HEAD_DIM)
    angles = frequency[:, None] * jnp.arange(tokens).astype(f32)[None, :]
    cosine, sine = jnp.cos(angles), jnp.sin(angles)

    out_t = out_weight.T
    decoder_peer = ladder.swap(decoder_weight, core)
    encoder_near, decoder_near = in_vmem(encoder_weight), in_vmem(decoder_weight)
    norms = jnp.sqrt(jnp.sum(jnp.square(decoder_weight.astype(f32)), axis=1) + epsilon)

    if paired:
        sends, keeps, squares = project(
            ladder, dp_steps[0], groups, heads, residual_t, norm_gain, query_weight, key_weight, value_weight
        )
    else:
        residual_float = residual_t.astype(f32)
        scaled = (residual_float * norm_gain[:, None]).astype(bf16)
        square = jnp.sum(residual_float * residual_float, axis=0, keepdims=True)
        pieces = []
        for g in range(groups):
            pieces += [
                query_weight[:, g * heads * HEAD_DIM : (g + 1) * heads * HEAD_DIM],
                key_weight[:, g * HEAD_DIM : (g + 1) * HEAD_DIM],
                value_weight[:, g * HEAD_DIM : (g + 1) * HEAD_DIM],
            ]
        stacked = jnp.concatenate(pieces, axis=1)
        projected = lax.dot_general(stacked, scaled, (((0,), (0,)), ((), ())), preferred_element_type=f32)
        sends, keeps, squares = [], [], []
        for cut in cuts:
            send = keep = projected[:, cut]
            if group_bits:
                half = send.shape[0] // 2
                up = ladder.bit(dp_steps[0]) == 1
                send, keep = jnp.where(up, keep[:half], keep[half:]), jnp.where(up, keep[half:], keep[:half])
            sends.append(jnp.concatenate([send.astype(bf16), split_rows(square[:, cut])], axis=0))
            keeps.append(keep)
            squares.append(square[:, cut])

    sends[0], sends[1], later = lax.optimization_barrier((sends[0], sends[1], residual_t))
    mine = share(later)
    steps = cores[1:] + routes[0]
    residual_own = ladder.gather(mine, steps[1:])
    residual_far = ladder.swap(residual_own, steps[0])
    old = ()
    attendeds = []
    errors, nears, hiddens, lows, slopes, activities = [], [], [], [], [], []
    for c in range(CHUNKS):
        send, part, square = sends[c], keeps[c], squares[c]
        for i, step in enumerate(dp_steps):
            got = ladder.swap(send, step)
            if i < len(dp_steps) - 1:
                send, part, square = advance(ladder, dp_steps[i + 1], i + 1 < group_bits, part, got, square)
        attended, *old = attend(c * width, heads, model_width, part, got, square, cosine, sine, *old)
        attendeds.append(attended)

    residuals = (residual_own, residual_far, ladder.swap(residual_own, core), ladder.swap(residual_far, core))
    if paired:
        residual_all = assemble(ladder, core, steps[0], ladder.order(cores + routes[0]), block, residuals)
    else:
        residual_all = canonical(residuals, steps, block)
        residual_all = [residual_all[:, cut] for cut in cuts]

    slots = [ladder.position(cores + routes[c % len(routes)]) * block for c in range(CHUNKS)]
    offsets = [lax.dynamic_slice_in_dim(decoder_bias, slot, block) for slot in slots]
    for c, attended in enumerate(attendeds):
        if paired:
            attended = ladder.gather(attended, group_steps[1:])
            got = ladder.swap(attended, group_steps[0])
            send, keep = project_out(ladder, group_steps[0], core, attended, got, out_t)
            packed = pack(ladder, core, keep, ladder.swap(send, core), post_gain)
        else:
            attended = ladder.gather(attended, group_steps)
            head = ladder.scatter(jnp.dot(out_t, attended, preferred_element_type=f32), cores, f32)
            packed = jnp.concatenate(
                [(head * gain).astype(bf16), split_rows(jnp.sum(head * head, axis=0, keepdims=True))], axis=0
            )
        steps = routes[c % len(routes)]
        path = cores[1:] + steps
        own = ladder.gather(packed, path[1:])
        if c == 1:
            own, norms, offsets, residual_all = lax.optimization_barrier((own, norms, offsets, residual_all))
        far = ladder.swap(own, path[0])
        pieces = own, far, ladder.swap(own, core), ladder.swap(far, core)
        near = (cores[1:] + steps)[0]
        kernel_block, places = block, ladder.order(cores + steps)
        if not paired:
            stride = block + EXTRA
            tails = sum(
                v[p * stride + block : (p + 1) * stride].astype(f32)
                for v in pieces
                for p in range(v.shape[0] // stride)
            )
            tails = split_rows(jnp.sum(tails, axis=0, keepdims=True))
            whole = cut_four(canonical(pieces, cores[1:] + steps, stride))
            pieces = [
                jnp.concatenate([v, tails if k == 0 else jnp.zeros_like(tails)], axis=0) for k, v in enumerate(whole)
            ]
            kernel_block, places = model_width // 4, ()
        slot, offset = slots[c], offsets[c]
        hidden, low, slope, activity, base = encode(
            ladder, core, cores + steps, places, kernel_block, pieces, residual_all[c], encoder_near, encoder_bias, offset
        )
        if not paired:
            base = base - lax.dynamic_slice_in_dim(hidden, slot, block, axis=0).astype(f32)
        send, part = decode(ladder, core, path[0], low, ladder.swap(low, core), decoder_near, decoder_peer)
        part = part + ladder.swap(send, path[0]).astype(f32)
        error = (ladder.scatter(part, path[1:], bf16) + base).astype(bf16)
        errors.append(ladder.quarters(error, core, cores[1:] + steps))
        nears.append(near)
        hiddens.append(hidden)
        lows.append(low)
        slopes.append(slope)
        activities.append(activity)

    encoder_grad, encoder_bias_grad, decoder_grad = gradients(
        ladder, core, nears, errors, hiddens, lows, slopes, activities, decoder_near, norms
    )
    return encoder_grad, encoder_bias_grad[0], decoder_grad


def solution(mesh):
    ladder = Ladder(mesh.shape["dp"], mesh.shape["mp"])
    placed = (
        P(None, "dp"),
        P("dp"),
        P("dp", "mp"),
        P("dp", "mp"),
        P("dp", "mp"),
        P("mp", "dp"),
        P("dp"),
        P(None, ("dp", "mp")),
        P(("dp", "mp")),
        P(("dp", "mp"), None),
        P(),
    )
    return jax.shard_map(
        functools.partial(on_device, ladder),
        mesh=mesh,
        in_specs=placed,
        out_specs=(P(None, ("dp", "mp")), P(("dp", "mp")), P(("dp", "mp"), None)),
        check_vma=False,
    )
```

```python
import functools

import jax
import jax.numpy as jnp
from jax import lax
from jax.experimental import pallas as pl
from jax.experimental.pallas import tpu as pltpu
from jax.sharding import PartitionSpec as P

HEAD_DIM = 128
CHUNKS = 2
EXTRA = 16

epsilon = 1e-06
softcap = 50.0
query_scale = 1.0 / 12.0
rope_base = 10000.0
smoothing = 0.1
penalty = 1.0
loss_weight = 0.0625

bf16 = jnp.bfloat16
f32 = jnp.float32
AXES = ("dp", "mp")


class Ladder:
    def __init__(self, dp, mp):
        self.dp, self.mp = dp, mp
        dp_bits, mp_bits = dp.bit_length() - 1, mp.bit_length() - 1
        assert dp == 1 << dp_bits and mp == 1 << mp_bits
        self.dp_bits = dp_bits
        self.cores = [(("mp", k), ("mp", k)) for k in range(mp_bits - 1, -1, -1)]

    def route(self, even, odd):
        if self.dp_bits < len(even):
            even = odd = tuple(range(self.dp_bits))
        rest = tuple(range(len(even), self.dp_bits))
        return [(("dp", j), ("dp", k)) for j, k in zip(even + rest, odd + rest)]

    def pairs(self, step):
        result = []
        for d in range(self.dp):
            for m in range(self.mp):
                axis, k = step[m & 1]
                peer = (d ^ (1 << k), m) if axis == "dp" else (d, m ^ (1 << k))
                result.append((d * self.mp + m, peer[0] * self.mp + peer[1]))
        return result

    def static_bit(self, step, d, m):
        axis, k = step[m & 1]
        return ((d if axis == "dp" else m) >> k) & 1

    def bit(self, step):
        d, m = lax.axis_index("dp"), lax.axis_index("mp")
        (axis, even), (_, odd) = step
        value = d if axis == "dp" else m
        if even == odd:
            return (value >> even) & 1
        return jnp.where(m & 1 == 0, (value >> even) & 1, (value >> odd) & 1)

    def swap(self, value, step):
        return lax.ppermute(value, AXES, self.pairs(step))

    def scatter(self, value, steps, wire):
        for step in steps:
            half = value.shape[0] // 2
            up = self.bit(step) == 1
            low, high = value[:half], value[half:]
            got = self.swap(jnp.where(up, low, high).astype(wire), step)
            value = jnp.where(up, high, low) + got.astype(f32)
        return value

    def gather(self, value, steps):
        for step in reversed(steps):
            got = self.swap(value, step)
            up = self.bit(step) == 1
            value = jnp.concatenate([jnp.where(up, got, value), jnp.where(up, value, got)], axis=0)
        return value

    def quarters(self, value, core, steps):
        own = self.gather(value, steps[1:])
        far = self.swap(own, steps[0])
        return own, far, self.swap(own, core), self.swap(far, core)

    def order(self, steps):
        where = {}
        for d in range(self.dp):
            for m in range(self.mp):
                p = 0
                for step in steps:
                    p = 2 * p + self.static_bit(step, d, m)
                where[p] = d * self.mp + m
        return [where[p] for p in range(self.dp * self.mp)]

    def position(self, steps):
        p = 0
        for step in steps:
            p = 2 * p + self.bit(step)
        return p

    def piece(self, core, step, k):
        up = self.bit(core)
        if k < 2:
            near = self.bit(step)
            return up, near if k == 0 else 1 - near
        d, m = lax.axis_index("dp"), lax.axis_index("mp") ^ (1 << core[0][1])
        (axis, even), (_, odd) = step
        value = d if axis == "dp" else m
        near = jnp.where(m & 1 == 0, (value >> even) & 1, (value >> odd) & 1)
        return 1 - up, near if k == 2 else 1 - near


VMEM = pl.BlockSpec(memory_space=pltpu.VMEM)


def in_hbm(value):
    return pltpu.with_memory_space_constraint(value, pltpu.HBM)


def in_vmem(value):
    return pltpu.with_memory_space_constraint(value, pltpu.VMEM)


SMALL = pltpu.CompilerParams(vmem_limit_bytes=6 << 20)


def aligned(index, size):
    return pl.ds(pl.multiple_of(index * size, size), size)


def square_rows(total, ref, first):
    high = total.astype(bf16).astype(f32)
    place = lax.broadcasted_iota(jnp.int32, (EXTRA, total.shape[1]), 0)
    rows = jnp.where(place == 0, high, jnp.where(place == 1, total - high, 0.0))
    ref[pl.ds(first, EXTRA), :] = rows.astype(bf16)


def column(ref, width):
    return jnp.broadcast_to(ref[...][None, :], (width, ref.shape[0])).T


def project_kernel(ladder, step, groups, heads, chunks, residual_ref, gain_ref, *refs):
    weights, outs = refs[:3], refs[3 : 3 + 3 * chunks]
    query_ref, key_ref, value_ref = refs[-4:-1]
    copies = [pltpu.make_async_copy(w, r, refs[-1].at[i]) for i, (w, r) in enumerate(zip(weights, refs[-4:-1]))]
    for copy in copies:
        copy.start()
    up = ladder.bit(step)
    tokens = residual_ref.shape[1]
    width = tokens // chunks
    wide = heads * HEAD_DIM
    residual = residual_ref[...].astype(f32)
    scaled = (residual * column(gain_ref, tokens)).astype(bf16)
    square = jnp.sum(residual * residual, axis=0, keepdims=True)
    for copy in copies:
        copy.wait()
    sends, keeps, squares = outs[:chunks], outs[chunks : 2 * chunks], outs[2 * chunks :]
    half = groups // 2

    def times(weight):
        return lax.dot_general(weight, scaled, (((0,), (0,)), ((), ())), preferred_element_type=f32)

    for refs, side in ((sends, 1 - up), (keeps, up)):
        for j in range(half):
            g = side * half + j
            first = j * (wide + 2 * HEAD_DIM)
            for weight, size in ((query_ref, wide), (key_ref, HEAD_DIM), (value_ref, HEAD_DIM)):
                value = times(weight[:, aligned(g, size)])
                for c, ref in enumerate(refs):
                    ref[pl.ds(first, size), :] = value[:, c * width : (c + 1) * width].astype(ref.dtype)
                first += size
    for c in range(chunks):
        part = square[:, c * width : (c + 1) * width]
        squares[c][...] = part
        square_rows(part, sends[c], half * (wide + 2 * HEAD_DIM))


def project(ladder, step, groups, heads, residual, gain, query, key, value):
    width = residual.shape[1] // CHUNKS
    rows = groups // 2 * (heads + 2) * HEAD_DIM
    shapes = (
        [jax.ShapeDtypeStruct((rows + EXTRA, width), bf16)] * CHUNKS
        + [jax.ShapeDtypeStruct((rows, width), f32)] * CHUNKS
        + [jax.ShapeDtypeStruct((1, width), f32)] * CHUNKS
    )
    outs = pl.pallas_call(
        functools.partial(project_kernel, ladder, step, groups, heads, CHUNKS),
        out_shape=shapes,
        in_specs=[VMEM] * 2 + [pl.BlockSpec(memory_space=pltpu.HBM)] * 3,
        scratch_shapes=[
            pltpu.VMEM(query.shape, bf16),
            pltpu.VMEM(key.shape, bf16),
            pltpu.VMEM(value.shape, bf16),
            pltpu.SemaphoreType.DMA((3,)),
        ],
        compiler_params=pltpu.CompilerParams(vmem_limit_bytes=10 << 20),
        cost_estimate=pl.CostEstimate(
            flops=4 * rows * residual.size, bytes_accessed=2 * (query.size + key.size + value.size), transcendentals=0
        ),
    )(residual, gain, in_hbm(query), in_hbm(key), in_hbm(value))
    return list(outs[:CHUNKS]), outs[CHUNKS : 2 * CHUNKS], outs[2 * CHUNKS :]


def step_kernel(ladder, step, halve, own_ref, got_ref, square_ref, send_ref, keep_ref, total_ref):
    rows, kept = own_ref.shape[0], keep_ref.shape[0]
    total = square_ref[...] + jnp.sum(got_ref[pl.ds(rows, EXTRA), :].astype(f32), axis=0, keepdims=True)
    total_ref[...] = total
    square_rows(total, send_ref, kept)
    if halve:
        up = ladder.bit(step)
        here, there = aligned(up, kept), aligned(1 - up, kept)
        send_ref[pl.ds(0, kept), :] = (own_ref[there, :] + got_ref[there, :].astype(f32)).astype(bf16)
        keep_ref[...] = own_ref[here, :] + got_ref[here, :].astype(f32)
    else:
        value = own_ref[...] + got_ref[pl.ds(0, rows), :].astype(f32)
        send_ref[pl.ds(0, kept), :] = value.astype(bf16)
        keep_ref[...] = value


def advance(ladder, step, halve, own, got, square):
    rows, width = own.shape
    kept = rows // 2 if halve else rows
    return pl.pallas_call(
        functools.partial(step_kernel, ladder, step, halve),
        out_shape=(
            jax.ShapeDtypeStruct((kept + EXTRA, width), bf16),
            jax.ShapeDtypeStruct((kept, width), f32),
            jax.ShapeDtypeStruct((1, width), f32),
        ),
        in_specs=[VMEM] * 3,
        compiler_params=SMALL,
        cost_estimate=pl.CostEstimate(flops=2 * own.size, bytes_accessed=12 * own.size, transcendentals=0),
    )(own, got, square)


def attention_kernel(start, heads, model_width, own_ref, got_ref, square_ref, cos_ref, sin_ref, *refs):
    oldk_ref, oldv_ref = refs[:2] if start else (None, None)
    out_ref, k_ref, v_ref = refs[-3:]
    width = own_ref.shape[1]
    half = HEAD_DIM // 2
    body = own_ref.shape[0]
    tail = jnp.sum(got_ref[pl.ds(body, EXTRA), :].astype(f32), axis=0, keepdims=True)
    inverse = lax.rsqrt((square_ref[...] + tail) / model_width + epsilon)
    lanes = pl.ds(start, width)
    cosine, sine = cos_ref[:, lanes], sin_ref[:, lanes]

    def rows(first, count):
        return (own_ref[pl.ds(first, count), :] + got_ref[pl.ds(first, count), :].astype(f32)) * inverse

    def rotated(first):
        front, back = rows(first, half), rows(first + half, half)
        return jnp.concatenate([front * cosine - back * sine, back * cosine + front * sine], axis=0).astype(bf16)

    base = heads * HEAD_DIM
    k_ref[:, pl.ds(start, width)] = rotated(base)
    v_ref[:, pl.ds(start, width)] = rows(base + HEAD_DIM, HEAD_DIM).astype(bf16)
    if start:
        k_ref[:, pl.ds(0, start)] = oldk_ref[...]
        v_ref[:, pl.ds(0, start)] = oldv_ref[...]
    keys, values = k_ref[...], v_ref[...]
    span = start + width
    allowed = lax.broadcasted_iota(jnp.int32, (span, width), 0) <= lax.broadcasted_iota(jnp.int32, (span, width), 1) + start
    for h in range(heads):
        query = rotated(h * HEAD_DIM)
        score = lax.dot_general(keys, query, (((0,), (0,)), ((), ())), preferred_element_type=f32) * query_scale
        capped = softcap * jnp.tanh(score / softcap)
        weights = jnp.where(allowed, jnp.exp(capped), 0.0)
        total = jnp.sum(weights, axis=0, keepdims=True)
        mixed = jnp.dot(values, weights.astype(bf16), preferred_element_type=f32)
        out_ref[pl.ds(h * HEAD_DIM, HEAD_DIM), :] = (mixed / total).astype(bf16)


def attend(start, heads, model_width, own, got, square, cosine, sine, *old):
    width = own.shape[1]
    span = start + width
    return pl.pallas_call(
        functools.partial(attention_kernel, start, heads, model_width),
        out_shape=(
            jax.ShapeDtypeStruct((heads * HEAD_DIM, width), bf16),
            jax.ShapeDtypeStruct((HEAD_DIM, span), bf16),
            jax.ShapeDtypeStruct((HEAD_DIM, span), bf16),
        ),
        compiler_params=SMALL,
        cost_estimate=pl.CostEstimate(
            flops=4 * heads * HEAD_DIM * span * width, bytes_accessed=8 * own.size, transcendentals=2 * heads * span * width
        ),
    )(own, got, square, cosine, sine, *old)


def out_kernel(ladder, near, core, own_ref, got_ref, weight_ref, send_ref, keep_ref):
    rows, columns = send_ref.shape[0], own_ref.shape[0]
    order, up = ladder.bit(near), ladder.bit(core)
    here, there = aligned(order, columns), aligned(1 - order, columns)
    for ref, half in ((send_ref, 1 - up), (keep_ref, up)):
        part = aligned(half, rows)
        ref[...] = jnp.dot(weight_ref[part, here], own_ref[...], preferred_element_type=f32) + jnp.dot(
            weight_ref[part, there], got_ref[...], preferred_element_type=f32
        )


def project_out(ladder, near, core, own, got, weight):
    shape = jax.ShapeDtypeStruct((weight.shape[0] // 2, own.shape[1]), f32)
    return pl.pallas_call(
        functools.partial(out_kernel, ladder, near, core),
        out_shape=(shape, shape),
        in_specs=[VMEM] * 3,
        compiler_params=SMALL,
        cost_estimate=pl.CostEstimate(
            flops=2 * weight.size * own.shape[1], bytes_accessed=2 * weight.size, transcendentals=0
        ),
    )(own, got, weight)


def pack_kernel(ladder, core, keep_ref, got_ref, gain_ref, packed_ref):
    head = keep_ref[...] + got_ref[...]
    rows, width = head.shape
    gain = column(gain_ref, width)
    gain = jnp.where(ladder.bit(core) == 1, gain[rows:], gain[:rows])
    packed_ref[pl.ds(0, rows), :] = (head * gain).astype(bf16)
    square_rows(jnp.sum(head * head, axis=0, keepdims=True), packed_ref, rows)


def pack(ladder, core, keep, got, gain):
    return pl.pallas_call(
        functools.partial(pack_kernel, ladder, core),
        out_shape=jax.ShapeDtypeStruct((keep.shape[0] + EXTRA, keep.shape[1]), bf16),
        in_specs=[VMEM] * 3,
        compiler_params=SMALL,
        cost_estimate=pl.CostEstimate(flops=4 * keep.size, bytes_accessed=10 * keep.size, transcendentals=0),
    )(keep, got, gain)


def targets(ladder, core, step, places, block, count, k):
    if not places:
        return [pl.ds((k * count + p) * block, block) for p in range(count)]
    side, near = ladder.piece(core, step, k)
    result = []
    for p in range(count):
        a, b, c, d = (places[q * count + p] for q in range(4))
        place = jnp.where(side == 0, jnp.where(near == 0, a, b), jnp.where(near == 0, c, d))
        result.append(aligned(place, block))
    return result


def assemble_kernel(ladder, core, step, places, block, *refs):
    count = refs[0].shape[0] // block
    width = refs[4].shape[1]
    for k in range(4):
        for p, target in enumerate(targets(ladder, core, step, places, block, count, k)):
            value = refs[k][pl.ds(p * block, block), :]
            for c, out_ref in enumerate(refs[4:]):
                out_ref[target, :] = value[:, c * width : (c + 1) * width]


def assemble(ladder, core, step, places, block, pieces):
    rows, width = pieces[0].shape
    return pl.pallas_call(
        functools.partial(assemble_kernel, ladder, core, step, places, block),
        out_shape=[jax.ShapeDtypeStruct((4 * rows, width // CHUNKS), bf16)] * CHUNKS,
        in_specs=[VMEM] * 4,
        compiler_params=pltpu.CompilerParams(vmem_limit_bytes=8 << 20),
        cost_estimate=pl.CostEstimate(flops=0, bytes_accessed=16 * rows * width, transcendentals=0),
    )(*pieces)


def encode_kernel(ladder, core, steps, places, block, model_width, *refs):
    pieces = refs[:4]
    residual_ref, enc_ref, bias_ref, offset_ref = refs[4:8]
    hidden_ref, low_ref, slope_ref, activity_ref, base_ref, hidden_buf, sems = refs[8:]
    width = pieces[0].shape[1]
    stride = block + EXTRA
    count = pieces[0].shape[0] // stride
    tail = jnp.zeros((EXTRA, width), f32)
    for ref in pieces:
        for p in range(count):
            tail = tail + ref[pl.ds(p * stride + block, EXTRA), :].astype(f32)
    inverse = lax.rsqrt(jnp.sum(tail, axis=0, keepdims=True) / model_width + epsilon)
    for k, ref in enumerate(pieces):
        for p, target in enumerate(targets(ladder, core, steps[1], places, block, count, k)):
            value = residual_ref[target, :].astype(f32) + ref[pl.ds(p * stride, block), :].astype(f32) * inverse
            hidden_buf[target, :] = value.astype(bf16)
    store = pltpu.make_async_copy(hidden_buf, hidden_ref, sems.at[0])
    store.start()
    if places:
        mine = hidden_buf[aligned(ladder.position(steps), block), :].astype(f32)
        base_ref[...] = column(offset_ref, width) - mine
    else:
        base_ref[...] = column(offset_ref, width)
    preact = lax.dot_general(enc_ref[...], hidden_buf[...], (((0,), (0,)), ((), ())), preferred_element_type=f32)
    scaled = (preact + column(bias_ref, width)) / smoothing
    active = smoothing * (jnp.maximum(scaled, 0.0) + jnp.log1p(jnp.exp(-jnp.abs(scaled))))
    low_ref[...] = active.astype(bf16)
    slope_ref[...] = jax.nn.sigmoid(scaled)
    activity_ref[...] = jnp.sum(active, axis=1, keepdims=True)
    store.wait()


def encode(ladder, core, steps, places, block, pieces, residual, encoder, bias, offset):
    width = pieces[0].shape[1]
    model_width, latents = encoder.shape
    hbm = pl.BlockSpec(memory_space=pltpu.HBM)
    return pl.pallas_call(
        functools.partial(encode_kernel, ladder, core, steps, places, block, model_width),
        out_shape=(
            jax.ShapeDtypeStruct((model_width, width), bf16),
            jax.ShapeDtypeStruct((latents, width), bf16),
            jax.ShapeDtypeStruct((latents, width), f32),
            jax.ShapeDtypeStruct((latents, 1), f32),
            jax.ShapeDtypeStruct((offset.shape[0], width), f32),
        ),
        in_specs=[VMEM] * 8,
        out_specs=[hbm] + [VMEM] * 4,
        scratch_shapes=[pltpu.VMEM((model_width, width), bf16), pltpu.SemaphoreType.DMA((1,))],
        compiler_params=pltpu.CompilerParams(vmem_limit_bytes=2 * encoder.size + 8 * model_width * width + (4 << 20)),
        cost_estimate=pl.CostEstimate(
            flops=2 * encoder.size * width, bytes_accessed=2 * encoder.size, transcendentals=4 * latents * width
        ),
    )(*pieces, residual, encoder, bias, offset)


def decode_kernel(ladder, core, step, low_ref, peer_low_ref, dec_ref, peer_dec_any, send_ref, keep_ref, buf, sems):
    up = ladder.bit(step)
    half = send_ref.shape[0]
    first = 2 * ladder.bit(core)
    loads = []
    for i, side in enumerate((1 - up, up)):
        loads.append(pltpu.make_async_copy(peer_dec_any.at[:, aligned(first + side, half)], buf.at[i], sems.at[i]))
        loads[-1].start()
    low, peer_low = low_ref[...], peer_low_ref[...]
    tile = half // 3
    for i, (ref, side) in enumerate(((send_ref, 1 - up), (keep_ref, up))):
        loads[i].wait()
        for t in range(3):
            rows = pl.ds(t * tile, tile)
            columns = pl.ds(pl.multiple_of((first + side) * half + t * tile, tile), tile)
            value = lax.dot_general(dec_ref[:, columns], low, (((0,), (0,)), ((), ())), preferred_element_type=f32)
            value = value + lax.dot_general(
                buf[i, :, rows], peer_low, (((0,), (0,)), ((), ())), preferred_element_type=f32
            )
            ref[rows, :] = value.astype(ref.dtype)


def decode(ladder, core, step, low, peer_low, decoder, peer_decoder):
    latents, width = low.shape
    half = decoder.shape[1] // 4
    hbm = pl.BlockSpec(memory_space=pltpu.HBM)
    return pl.pallas_call(
        functools.partial(decode_kernel, ladder, core, step),
        out_shape=(jax.ShapeDtypeStruct((half, width), bf16), jax.ShapeDtypeStruct((half, width), f32)),
        in_specs=[VMEM] * 3 + [hbm],
        scratch_shapes=[pltpu.VMEM((2, latents, half), bf16), pltpu.SemaphoreType.DMA((2,))],
        compiler_params=pltpu.CompilerParams(vmem_limit_bytes=2 * decoder.size + 6 * half * width + (6 << 20)),
        cost_estimate=pl.CostEstimate(
            flops=4 * decoder.size * width, bytes_accessed=4 * decoder.size, transcendentals=0
        ),
    )(low, peer_low, decoder, in_hbm(peer_decoder))


def final_kernel(ladder, core, steps, *refs):
    chunks = CHUNKS
    errors = [refs[4 * c : 4 * c + 4] for c in range(chunks)]
    refs = refs[4 * chunks :]
    hidden_any, low, slope, activity = (refs[i * chunks : (i + 1) * chunks] for i in range(4))
    dec_ref, norm_ref, enc_out, bias_ref, dec_out = refs[4 * chunks : 4 * chunks + 5]
    hidden, error, enc_buf, dec_buf, in_sem, enc_sem, dec_sem = refs[4 * chunks + 5 :]
    width = hidden_any[0].shape[1]
    loads = []
    for c in range(chunks):
        place = hidden.at[:, pl.ds(c * width, width)]
        loads.append(pltpu.make_async_copy(hidden_any[c], place, in_sem.at[c]))
        loads[-1].start()
    quarter = errors[0][0].shape[0]
    for c in range(chunks):
        for k in range(4):
            side, near = ladder.piece(core, steps[c], k)
            error[aligned(2 * side + near, quarter), pl.ds(c * width, width)] = errors[c][k][...]
    lows = jnp.concatenate([ref[...] for ref in low], axis=1)
    slopes = jnp.concatenate([ref[...] for ref in slope], axis=1)
    norms = column(norm_ref, 128)[:, :1]
    copies = []

    def send(buf, out, index, sem):
        copies.append(pltpu.make_async_copy(buf.at[index], out.at[index], sem))
        copies[-1].start()

    tile = hidden.shape[0] // 9
    ratio = loss_weight * penalty * sum(ref[...] for ref in activity) / norms
    for t in range(9):
        columns = pl.ds(t * tile, tile)
        outer = lax.dot_general(lows, error[columns, :], (((1,), (1,)), ((), ())), preferred_element_type=f32)
        dec_buf[:, columns] = (2.0 * loss_weight * outer + ratio * dec_ref[:, columns].astype(f32)).astype(bf16)
    send(dec_buf, dec_out, slice(None), dec_sem.at[0])
    feedback = jnp.dot(dec_ref[...], error[...], preferred_element_type=f32)
    turned = (loss_weight * (2.0 * feedback + penalty * norms) * slopes).T
    bias_ref[...] = jnp.sum(turned, axis=0, keepdims=True)
    turned = turned.astype(bf16)
    for load in loads:
        load.wait()
    for t in range(9):
        rows = pl.ds(t * tile, tile)
        enc_buf[rows, :] = jnp.dot(hidden[rows, :], turned, preferred_element_type=f32).astype(bf16)
        send(enc_buf, enc_out, (rows, slice(None)), enc_sem.at[t])
    for copy in copies:
        copy.wait()


def gradients(ladder, core, steps, errors, hidden, low, slope, activity, decoder, norms):
    latents, model_width = decoder.shape
    tokens = CHUNKS * hidden[0].shape[1]
    hbm = pl.BlockSpec(memory_space=pltpu.HBM)
    flat = [piece for pieces in errors for piece in pieces]
    return pl.pallas_call(
        functools.partial(final_kernel, ladder, core, steps),
        out_shape=(
            jax.ShapeDtypeStruct((model_width, latents), bf16),
            jax.ShapeDtypeStruct((1, latents), f32),
            jax.ShapeDtypeStruct((latents, model_width), bf16),
        ),
        in_specs=[VMEM] * len(flat) + [hbm] * CHUNKS + [VMEM] * (3 * CHUNKS + 2),
        out_specs=(hbm, VMEM, hbm),
        scratch_shapes=[
            pltpu.VMEM((model_width, tokens), bf16),
            pltpu.VMEM((model_width, tokens), bf16),
            pltpu.VMEM((model_width, latents), bf16),
            pltpu.VMEM((latents, model_width), bf16),
            pltpu.SemaphoreType.DMA((CHUNKS,)),
            pltpu.SemaphoreType.DMA((9,)),
            pltpu.SemaphoreType.DMA((1,)),
        ],
        compiler_params=pltpu.CompilerParams(
            vmem_limit_bytes=4 * decoder.size + 4 * model_width * tokens + (6 << 20)
        ),
        cost_estimate=pl.CostEstimate(
            flops=6 * decoder.size * tokens, bytes_accessed=12 * decoder.size, transcendentals=0
        ),
    )(*flat, *hidden, *low, *slope, *activity, decoder, norms)


def split_rows(value):
    high = lax.reduce_precision(value, 8, 7)
    rows = jnp.concatenate([high, value - high], axis=0).astype(bf16)
    return jnp.concatenate([rows, jnp.zeros((EXTRA - 2, value.shape[1]), bf16)], axis=0)


def on_device(ladder, residual, norm_gain, query_weight, key_weight, value_weight, out_weight, post_gain,
              encoder_weight, encoder_bias, decoder_weight, decoder_bias):
    tokens = residual.shape[0]
    model_width = decoder_weight.shape[1]
    groups = key_weight.shape[1] // HEAD_DIM
    heads = query_weight.shape[1] // key_weight.shape[1]
    width = tokens // CHUNKS
    cuts = [slice(c * width, (c + 1) * width) for c in range(CHUNKS)]

    cores = ladder.cores
    dp_steps = ladder.route((0, 1, 2), (1, 0, 2))
    routes = [ladder.route((0, 1, 2), (1, 2, 0)), ladder.route((2, 0, 1), (1, 0, 2))]
    group_bits = groups.bit_length() - 1
    assert groups == 1 << group_bits and group_bits <= len(dp_steps)
    group_steps, copy_steps = dp_steps[:group_bits], dp_steps[group_bits:]

    residual_t = residual.T
    core = cores[0]
    core_bit = ladder.bit(core)
    paired = len(cores) == 1 and residual_t.shape[0] % 32 == 0 and group_bits >= 1

    def share(value):
        for step in cores:
            half = value.shape[0] // 2
            value = jnp.where(ladder.bit(step) == 1, value[half:], value[:half])
        return value

    gain = share(post_gain[:, None])
    block = gain.shape[0]

    def canonical(pieces, steps, stride):
        own, far, own_peer, far_peer = pieces
        value = []
        for k, (a, b) in ((0, (own, far)), (2, (own_peer, far_peer))):
            _, near = ladder.piece(core, steps[0], k)
            value.append(jnp.concatenate([jnp.where(near == 1, b, a), jnp.where(near == 1, a, b)], axis=0))
        own, got = value
        value = jnp.concatenate([jnp.where(core_bit == 1, got, own), jnp.where(core_bit == 1, own, got)], axis=0)
        order = ladder.order(cores[:1] + steps)
        return jnp.concatenate(
            [value[p * stride : p * stride + block] for p in (order.index(i) for i in range(len(order)))], axis=0
        )

    def cut_four(value):
        quarter = value.shape[0] // 4
        return [value[k * quarter : (k + 1) * quarter] for k in range(4)]

    half_dim = HEAD_DIM // 2
    frequency = rope_base ** (-2.0 * jnp.arange(half_dim, dtype=f32) / HEAD_DIM)
    angles = frequency[:, None] * jnp.arange(tokens).astype(f32)[None, :]
    cosine, sine = jnp.cos(angles), jnp.sin(angles)

    out_t = out_weight.T
    decoder_peer = ladder.swap(decoder_weight, core)
    encoder_near, decoder_near = in_vmem(encoder_weight), in_vmem(decoder_weight)
    norms = jnp.sqrt(jnp.sum(jnp.square(decoder_weight.astype(f32)), axis=1) + epsilon)

    if paired:
        sends, keeps, squares = project(
            ladder, dp_steps[0], groups, heads, residual_t, norm_gain, query_weight, key_weight, value_weight
        )
    else:
        residual_float = residual_t.astype(f32)
        scaled = (residual_float * norm_gain[:, None]).astype(bf16)
        square = jnp.sum(residual_float * residual_float, axis=0, keepdims=True)
        pieces = []
        for g in range(groups):
            pieces += [
                query_weight[:, g * heads * HEAD_DIM : (g + 1) * heads * HEAD_DIM],
                key_weight[:, g * HEAD_DIM : (g + 1) * HEAD_DIM],
                value_weight[:, g * HEAD_DIM : (g + 1) * HEAD_DIM],
            ]
        stacked = jnp.concatenate(pieces, axis=1)
        projected = lax.dot_general(stacked, scaled, (((0,), (0,)), ((), ())), preferred_element_type=f32)
        sends, keeps, squares = [], [], []
        for cut in cuts:
            send = keep = projected[:, cut]
            if group_bits:
                half = send.shape[0] // 2
                up = ladder.bit(dp_steps[0]) == 1
                send, keep = jnp.where(up, keep[:half], keep[half:]), jnp.where(up, keep[half:], keep[:half])
            sends.append(jnp.concatenate([send.astype(bf16), split_rows(square[:, cut])], axis=0))
            keeps.append(keep)
            squares.append(square[:, cut])

    sends[0], sends[1], later = lax.optimization_barrier((sends[0], sends[1], residual_t))
    mine = share(later)
    spread = ladder.route((0, 1, 2), (1, 0, 2))
    steps = cores[1:] + spread
    residual_own = ladder.gather(mine, steps[1:])
    residual_far = ladder.swap(residual_own, steps[0])
    old = ()
    attendeds = []
    errors, nears, hiddens, lows, slopes, activities = [], [], [], [], [], []
    for c in range(CHUNKS):
        send, part, square = sends[c], keeps[c], squares[c]
        for i, step in enumerate(dp_steps):
            got = ladder.swap(send, step)
            if i < len(dp_steps) - 1:
                send, part, square = advance(ladder, dp_steps[i + 1], i + 1 < group_bits, part, got, square)
        attended, *old = attend(c * width, heads, model_width, part, got, square, cosine, sine, *old)
        attendeds.append(attended)

    residuals = (residual_own, residual_far, ladder.swap(residual_own, core), ladder.swap(residual_far, core))
    if paired:
        residual_all = assemble(ladder, core, steps[0], ladder.order(cores + spread), block, residuals)
    else:
        residual_all = canonical(residuals, steps, block)
        residual_all = [residual_all[:, cut] for cut in cuts]

    slots = [ladder.position(cores + routes[c % len(routes)]) * block for c in range(CHUNKS)]
    offsets = [lax.dynamic_slice_in_dim(decoder_bias, slot, block) for slot in slots]
    for c, attended in enumerate(attendeds):
        if paired:
            attended = ladder.gather(attended, group_steps[1:])
            got = ladder.swap(attended, group_steps[0])
            send, keep = project_out(ladder, group_steps[0], core, attended, got, out_t)
            packed = pack(ladder, core, keep, ladder.swap(send, core), post_gain)
        else:
            attended = ladder.gather(attended, group_steps)
            head = ladder.scatter(jnp.dot(out_t, attended, preferred_element_type=f32), cores, f32)
            packed = jnp.concatenate(
                [(head * gain).astype(bf16), split_rows(jnp.sum(head * head, axis=0, keepdims=True))], axis=0
            )
        steps = routes[c % len(routes)]
        path = cores[1:] + steps
        own = ladder.gather(packed, path[1:])
        if c == 1:
            own, norms, offsets, residual_all = lax.optimization_barrier((own, norms, offsets, residual_all))
        far = ladder.swap(own, path[0])
        pieces = own, far, ladder.swap(own, core), ladder.swap(far, core)
        near = (cores[1:] + steps)[0]
        kernel_block, places = block, ladder.order(cores + steps)
        if not paired:
            stride = block + EXTRA
            tails = sum(
                v[p * stride + block : (p + 1) * stride].astype(f32)
                for v in pieces
                for p in range(v.shape[0] // stride)
            )
            tails = split_rows(jnp.sum(tails, axis=0, keepdims=True))
            whole = cut_four(canonical(pieces, cores[1:] + steps, stride))
            pieces = [
                jnp.concatenate([v, tails if k == 0 else jnp.zeros_like(tails)], axis=0) for k, v in enumerate(whole)
            ]
            kernel_block, places = model_width // 4, ()
        slot, offset = slots[c], offsets[c]
        hidden, low, slope, activity, base = encode(
            ladder, core, cores + steps, places, kernel_block, pieces, residual_all[c], encoder_near, encoder_bias, offset
        )
        if not paired:
            base = base - lax.dynamic_slice_in_dim(hidden, slot, block, axis=0).astype(f32)
        send, part = decode(ladder, core, path[0], low, ladder.swap(low, core), decoder_near, decoder_peer)
        part = part + ladder.swap(send, path[0]).astype(f32)
        error = (ladder.scatter(part, path[1:], bf16) + base).astype(bf16)
        errors.append(ladder.quarters(error, core, cores[1:] + steps))
        nears.append(near)
        hiddens.append(hidden)
        lows.append(low)
        slopes.append(slope)
        activities.append(activity)

    encoder_grad, encoder_bias_grad, decoder_grad = gradients(
        ladder, core, nears, errors, hiddens, lows, slopes, activities, decoder_near, norms
    )
    return encoder_grad, encoder_bias_grad[0], decoder_grad


def solution(mesh):
    ladder = Ladder(mesh.shape["dp"], mesh.shape["mp"])
    placed = (
        P(None, "dp"),
        P("dp"),
        P("dp", "mp"),
        P("dp", "mp"),
        P("dp", "mp"),
        P("mp", "dp"),
        P("dp"),
        P(None, ("dp", "mp")),
        P(("dp", "mp")),
        P(("dp", "mp"), None),
        P(),
    )
    return jax.shard_map(
        functools.partial(on_device, ladder),
        mesh=mesh,
        in_specs=placed,
        out_specs=(P(None, ("dp", "mp")), P(("dp", "mp")), P(("dp", "mp"), None)),
        check_vma=False,
    )
```
